256 devices in a mesh: col: 32 (over z, x), bin: 8 (over y, core).
Axes of the slice: x: 4, y: 4, z: 8, core: 2. Of those that a mesh axis runs over, the one named last changes fastest.
Arguments:
- slope: float32 [262144], P('bin'), may hold values from -6 to 6
- curvature: float32 [262144], P('bin'), may hold values from -6 to 0
- target_mean: float32 [262144], P('bin'), may hold values from 0.15 to 0.85
- target_var: float32 [262144], P('bin'), may hold values from 0.06 to 0.12
- table: float32 [64, 512], P(None, 'col'), may hold values from -6 to 6
Outputs:
- species_mean: float32 [64, 262144], P('col')
- final_slope: float32 [262144], replicated
The draws below stay inside these ranges and needn't reach their ends.
All inputs are finite; a program needn't handle non-finite values.
Results may differ from the reference program's by a relative error of at most 0.0001.
Values sent between devices are 32-bit elements; how exact they have to be, the bound alone decides.
No kernel may reach another device: no remote copies, remote signals or barrier semaphores. Data moves between devices by JAX's collectives and lax.ppermute only.
A program may use at most 64 MiB of HBM per device.

```python
import math
import jax
import jax.numpy as jnp
from jax import lax

CPTS = 512
SPECIES = 64
ITERS = 3
BINS = 262144


def block_levels(rng, shape, split, smallest, top_value):
    def one(axis_at, blocks):
        heights = jax.random.uniform(jax.random.fold_in(jax.random.fold_in(rng, 6), axis_at), (blocks,), jnp.float32, smallest / len(split), top_value / len(split))
        return jnp.repeat(jnp.exp(heights), shape[axis_at] // blocks).reshape((-1,) + (1,) * (len(shape) - axis_at - 1))

    factor_of = one(*split[0])
    for cut in split[1:]:
        factor_of = factor_of * one(*cut)
    return factor_of


def gaussian(key, shape, spread, bound, pieces=(), dtype=jnp.bfloat16):
    level = block_levels(key, shape, pieces, -0.22, 0.18) if pieces else 1.0
    result = jax.random.normal(key, shape, jnp.float32) * spread * level
    return jnp.minimum(jnp.maximum(result, -bound), bound).astype(dtype)


def setup_inputs(seed: int = 0) -> dict:
    key_list = jax.random.split(jax.random.key(seed), 6)
    return {
        "slope": jnp.clip(jax.random.uniform(key_list[0], (BINS,), jnp.float32, -6.0, 6.0) * block_levels(key_list[0], (BINS,), ((0, 8),), -0.4, 0.0), -6.0, 6.0),
        "curvature": jnp.clip(-6.0 + 6.0 * jax.random.uniform(key_list[1], (BINS,), jnp.float32) ** block_levels(key_list[1], (BINS,), ((0, 8),), -0.2, 0.2), -6.0, 0.0),
        "target_mean": jnp.clip(0.15 + 0.70000002 * jax.random.uniform(key_list[2], (BINS,), jnp.float32) ** block_levels(key_list[2], (BINS,), ((0, 8),), -0.2, 0.2), 0.15, 0.85),
        "target_var": jnp.clip(0.06 + 0.06 * jax.random.uniform(key_list[3], (BINS,), jnp.float32) ** block_levels(key_list[3], (BINS,), ((0, 8),), -0.2, 0.2), 0.06, 0.12),
        "table": gaussian(key_list[4], (SPECIES, CPTS), 1.0, 6.0, ((1, 32),), jnp.float32),
    }


def solve_block(items):
    slope, curvature, target_mean, target_var, table = items
    points = ((jnp.arange(CPTS).astype(jnp.float32) + 0.5) / CPTS)[:, None]
    lam = slope
    for step in range(ITERS):
        expo = jnp.exp(lam[None, :] * points + curvature[None, :] * points * points)
        partition = jnp.sum(expo, axis=0)
        moment = jnp.sum(points * expo, axis=0)
        lam = lam + (target_mean - moment / partition) / target_var
    expo = jnp.exp(lam[None, :] * points + curvature[None, :] * points * points)
    total = jnp.sum(expo, axis=0)
    weights = expo / total[None, :]
    values = jnp.dot(table, weights, precision=lax.Precision.HIGHEST, preferred_element_type=jnp.float32)
    return values, lam


def reference(slope, curvature, target_mean, target_var, table):
    block = math.gcd(BINS, 4096)
    count = BINS // block

    def one(items):
        return solve_block((items[0], items[1], items[2], items[3], table))

    stacked = (slope.reshape(count, block), curvature.reshape(count, block),
               target_mean.reshape(count, block), target_var.reshape(count, block))
    values, lam = lax.map(one, stacked)
    species_mean = jnp.transpose(values, (1, 0, 2)).reshape(SPECIES, BINS)
    return species_mean, lam.reshape(BINS)
```

```python
import functools

import jax
import jax.numpy as jnp
from jax import lax
from jax.experimental import pallas as pl
from jax.experimental.pallas import tpu as pltpu
from jax.sharding import PartitionSpec as P

ITERS = 3
CHUNKS = 2
LANES = 128
COARSE = 8
FINE = 16


def newton_kernel(x_ref, slope_ref, curve_ref, mean_ref, var_ref, lam_ref, ch_ref, sh_ref, g_ref):
    per_chunk = lam_ref.shape[1] // 8

    def body(v, _):
        chunk = v // per_chunk
        rows = pl.ds(pl.multiple_of((v % per_chunk) * 8, 8), 8)
        curve = curve_ref[chunk, 0, rows, :]
        mean = mean_ref[chunk, 0, rows, :]
        inverse = 1.0 / var_ref[chunk, 0, rows, :]
        for j in range(FINE):
            angle = curve * ((2 * j + 1) / 16384.0)
            up, down = jnp.exp(angle), jnp.exp(-angle)
            up2, down2 = up * up, down * down
            for i in range(COARSE):
                ch_ref[i * FINE + j] = 0.5 * (up + down)
                sh_ref[i * FINE + j] = 0.5 * (up - down)
                if i < COARSE - 1:
                    up, down = up * up2, down * down2
            g_ref[j] = jnp.exp(curve * (((2 * j + 1) / 1024.0) ** 2))
        for i in range(COARSE):
            g_ref[FINE + i] = jnp.exp(curve * (((2 * i + 1) / 32.0) ** 2))

        def newton(_, lam):
            mu = lam + curve
            up, down = jnp.exp(mu * (1 / 1024.0)), jnp.exp(mu * (-1 / 1024.0))
            up2, down2 = up * up, down * down
            sums = [[None] * 4 for _ in range(COARSE)]
            for j in range(FINE):
                g = g_ref[j]
                even, odd = g * (up + down), g * (up - down)
                d = (2 * j + 1) / 1024.0
                d_even, d_odd = even * d, odd * d
                for i in range(COARSE):
                    ch, sh = ch_ref[i * FINE + j], sh_ref[i * FINE + j]
                    terms = (ch * even, sh * odd, ch * d_odd, sh * d_even)
                    sums[i] = [t if s is None else s + t for s, t in zip(sums[i], terms)]
                if j < FINE - 1:
                    up, down = up * up2, down * down2
            up, down = jnp.exp(mu * (1 / 32.0)), jnp.exp(mu * (-1 / 32.0))
            up2, down2 = up * up, down * down
            partition, moment = 0.0, 0.0
            for i in range(COARSE):
                g = g_ref[FINE + i]
                even, odd = g * (up + down), g * (up - down)
                a = (2 * i + 1) / 32.0
                e0, o0, o1, e1 = sums[i]
                partition = partition + (even * e0 + odd * o0)
                moment = moment + (a * (odd * e0 + even * o0) + (even * o1 + odd * e1))
                if i < COARSE - 1:
                    up, down = up * up2, down * down2
            return lam + (mean - (0.5 + moment / partition)) * inverse

        lam_ref[chunk, rows, :] = lax.fori_loop(0, ITERS, newton, slope_ref[chunk, 0, rows, :])
        return 0

    lax.fori_loop(0, CHUNKS * per_chunk, body, 0)


def newton(x, slope, curve, mean, var):
    rows = slope.shape[2]
    mine = pl.BlockSpec((CHUNKS, 1, rows, LANES), lambda g, x: (0, x[0], 0, 0))
    return pl.pallas_call(
        newton_kernel,
        out_shape=jax.ShapeDtypeStruct((CHUNKS, rows, LANES), jnp.float32),
        grid_spec=pltpu.PrefetchScalarGridSpec(
            num_scalar_prefetch=1,
            grid=(1,),
            in_specs=[mine] * 4,
            out_specs=pl.BlockSpec((CHUNKS, rows, LANES), lambda g, x: (0, 0, 0)),
            scratch_shapes=[
                pltpu.VMEM((COARSE * FINE, 8, LANES), jnp.float32),
                pltpu.VMEM((COARSE * FINE, 8, LANES), jnp.float32),
                pltpu.VMEM((COARSE + FINE, 8, LANES), jnp.float32),
            ],
        ),
        cost_estimate=pl.CostEstimate(flops=8192 * 512 * 12, bytes_accessed=1 << 18, transcendentals=0),
        name="newton",
    )(x, slope, curve, mean, var)


def species_kernel(x_ref, lam_ref, curve_ref, table_ref, *refs):
    outs, (turned_ref,) = refs[:-1], refs[-1:]
    turned_ref[...] = jnp.transpose(table_ref[...])
    table = jnp.concatenate([turned_ref[pl.ds(p, 8, stride=16), :] for p in range(16)], axis=1)
    high = table.astype(jnp.bfloat16)
    low = (table - high.astype(jnp.float32)).astype(jnp.bfloat16)
    row = lax.broadcasted_iota(jnp.int32, (8, 8), 0)
    column = lax.broadcasted_iota(jnp.int32, (8, 8), 1)
    order = jnp.where(column == 2 * ((row // 2) ^ x_ref[0]) + row % 2, 1.0, 0.0).astype(jnp.bfloat16)
    parts = [jnp.dot(order, part, preferred_element_type=jnp.float32) for part in (high, low)]
    ones = jnp.ones((16, table.shape[1]), jnp.float32)
    left = jnp.concatenate([*parts, ones], axis=0).astype(jnp.bfloat16)
    sub = lax.broadcasted_iota(jnp.int32, (8, LANES), 0).astype(jnp.float32)

    def tile(row):
        lam = jnp.broadcast_to(lam_ref[0, pl.ds(row, 1), :], (8, LANES))
        curve = jnp.broadcast_to(curve_ref[0, 0, pl.ds(row, 1), :], (8, LANES))
        mu = lam + curve
        ratio2 = jnp.exp(curve * (2.0 / (512.0 * 512.0)))
        columns = []
        for g in range(4):
            s = ((sub + 8.0 * g) * 16.0 + 0.5) * (1 / 512.0) - 0.5
            e = jnp.exp(mu * s + curve * (s * s))
            ratio = jnp.exp(mu * (1 / 512.0) + curve * ((2.0 * s + 1 / 512.0) * (1 / 512.0)))
            column = []
            for p in range(16):
                column.append(e)
                if p < 15:
                    e = e * ratio
                    ratio = ratio * ratio2
            columns.append(column)
        return jnp.concatenate([columns[g][p] for p in range(16) for g in range(4)], axis=0)

    def body(t, _):
        e = jnp.concatenate([tile(2 * t), tile(2 * t + 1)], axis=1)
        e_high = e.astype(jnp.bfloat16)
        e_low = (e - e_high.astype(jnp.float32)).astype(jnp.bfloat16)
        sums = jnp.dot(left, e_high, preferred_element_type=jnp.float32)
        sums = sums + jnp.dot(left, e_low, preferred_element_type=jnp.float32)
        values = (sums[0:8] + sums[8:16]) / sums[16:24]
        lanes = pl.ds(pl.multiple_of(t * 2 * LANES, 2 * LANES), 2 * LANES)
        for d, out in enumerate(outs):
            out[:, lanes] = values[2 * d : 2 * d + 2]
        return 0

    lax.fori_loop(0, lam_ref.shape[1] // 2, body, 0)


def species(x, lam, curve, table, chunk):
    rows = lam.shape[1]
    bins = rows * LANES
    return pl.pallas_call(
        species_kernel,
        out_shape=[jax.ShapeDtypeStruct((2, bins), jnp.float32)] * 4,
        grid_spec=pltpu.PrefetchScalarGridSpec(
            num_scalar_prefetch=1,
            grid=(1,),
            in_specs=[
                pl.BlockSpec((1, rows, LANES), lambda g, x: (chunk, 0, 0)),
                pl.BlockSpec((1, 1, rows, LANES), lambda g, x: (chunk, x[0], 0, 0)),
                pl.BlockSpec((32, LANES), lambda g, x: (0, 0)),
            ],
            out_specs=[pl.BlockSpec((2, bins), lambda g, x: (0, 0))] * 4,
            scratch_shapes=[pltpu.VMEM((LANES, 32), jnp.float32)],
        ),
        cost_estimate=pl.CostEstimate(flops=bins * 512 * 80, bytes_accessed=bins * 40, transcendentals=0),
        name="species",
    )(x, lam, curve, table)


def join_kernel(x_ref, *refs):
    pieces, out = refs[:4], refs[4]
    width = pieces[0].shape[1]
    for d in range(4):
        out[:, pl.ds(pl.multiple_of((x_ref[0] ^ d) * width, LANES), width)] = pieces[d][...]


def join(x, pieces):
    height, width = pieces[0].shape
    return pl.pallas_call(
        join_kernel,
        out_shape=jax.ShapeDtypeStruct((height, 4 * width), jnp.float32),
        in_specs=[pl.BlockSpec(memory_space=pltpu.SMEM)] + [pl.BlockSpec(memory_space=pltpu.VMEM)] * 4,
        out_specs=pl.BlockSpec(memory_space=pltpu.VMEM),
        name="join",
    )(x, *pieces)


def lay_kernel(place_ref, *refs):
    n = 8 * CHUNKS
    species_in, lam_in = refs[:n], refs[n : n + 8]
    species_out, lam_out, sems = refs[n + 8 :]
    copies = []
    width = species_in[0].shape[1]
    for k in range(8):
        group = place_ref[0] ^ k
        length = lam_in[k].shape[0]
        copies.append((lam_in[k], lam_out.at[pl.ds(pl.multiple_of(group * length, 8), length), :]))
        for chunk in range(CHUNKS):
            start = pl.multiple_of((group * CHUNKS + chunk) * width, LANES)
            copies.append((species_in[chunk * 8 + k], species_out.at[:, pl.ds(start, width)]))
    started = [pltpu.make_async_copy(a, b, sems.at[i]) for i, (a, b) in enumerate(copies)]
    for copy in started:
        copy.start()
    for copy in started:
        copy.wait()


def lay(place, species_blocks, lam_blocks):
    anywhere = pl.BlockSpec(memory_space=pl.ANY)
    n = 8 * CHUNKS
    height, width = species_blocks[0].shape
    rows = lam_blocks[0].shape[0]
    return pl.pallas_call(
        lay_kernel,
        out_shape=[
            jax.ShapeDtypeStruct((height, n * width), jnp.float32),
            jax.ShapeDtypeStruct((8 * rows, LANES), jnp.float32),
        ],
        in_specs=[pl.BlockSpec(memory_space=pltpu.SMEM)] + [anywhere] * (n + 8),
        out_specs=[anywhere] * 2,
        scratch_shapes=[pltpu.SemaphoreType.DMA((n + 8,))],
        name="lay",
    )(place, *species_blocks, *lam_blocks)


def swap(array, axis, bit):
    size = lax.axis_size(axis)
    return lax.ppermute(array, axis, [(i, i ^ bit) for i in range(size)])


def spread(block):
    own = [block] + [swap(block, "bin", 2 * e) for e in (1, 3, 2)]
    other = [swap(b, "bin", 1) for b in own]
    order = {0: 0, 2: 1, 6: 2, 4: 3}
    return [(other if k % 2 else own)[order[k - k % 2]] for k in range(8)]


def per_device(slope, curvature, target_mean, target_var, table):
    column = lax.axis_index("col")
    x = jnp.reshape(column % 4, (1,)).astype(jnp.int32)
    place = jnp.reshape(lax.axis_index("bin"), (1,)).astype(jnp.int32)
    columns = lax.axis_size("col")
    sent = jnp.broadcast_to(table.reshape(8, 1, 8 * 16), (8, 4, 8 * 16)).reshape(columns, 8 * 16)
    points = lax.all_to_all(sent, "col", split_axis=0, concat_axis=0, tiled=True)

    bins = slope.shape[0]
    rows = bins // (CHUNKS * 4 * LANES)
    args = [a.reshape(CHUNKS, 4, rows, LANES) for a in (slope, curvature, target_mean, target_var)]
    lam = newton(x, *args)
    lam_pieces = [lam.reshape(1, -1)] + [swap(lam, "col", d).reshape(1, -1) for d in (1, 2, 3)]
    flat = [p.reshape(CHUNKS, rows * LANES) for p in lam_pieces]
    lam_block = join(x, flat)
    lam_block = lam_block.reshape(bins // LANES, LANES)
    lam_blocks = spread(lam_block)

    blocks = []
    for chunk in range(CHUNKS):
        pieces = species(x, lam, args[1], points, chunk)
        pieces = [pieces[0]] + [swap(pieces[d], "col", d) for d in (1, 2, 3)]
        blocks += spread(join(x, pieces))
    species_mean, final_slope = lay(place, blocks, lam_blocks)
    return species_mean, final_slope.reshape(-1)


def solution(mesh):
    placed = (P("bin"), P("bin"), P("bin"), P("bin"), P(None, "col"))
    return jax.shard_map(
        per_device, mesh=mesh, in_specs=placed, out_specs=(P("col", None), P()), check_vma=False
    )
```

```python
import jax
import jax.numpy as jnp
import numpy as np
from jax import lax
from jax.experimental import pallas as pl
from jax.experimental.pallas import tpu as pltpu
from jax.sharding import PartitionSpec as P

ITERS = 3
CHUNKS = 1
LANES = 128
COARSE = 8
FINE = 16


def newton_kernel(x_ref, slope_ref, curve_ref, mean_ref, var_ref, lam_ref, ch_ref, sh_ref, g_ref):
    per_chunk = lam_ref.shape[1] // 8

    def body(v, _):
        chunk = v // per_chunk
        rows = pl.ds(pl.multiple_of((v % per_chunk) * 8, 8), 8)
        curve = curve_ref[chunk, 0, rows, :]
        mean = mean_ref[chunk, 0, rows, :]
        inverse = 1.0 / var_ref[chunk, 0, rows, :]
        for j in range(FINE):
            angle = curve * ((2 * j + 1) / 16384.0)
            up, down = jnp.exp(angle), jnp.exp(-angle)
            up2, down2 = up * up, down * down
            for i in range(COARSE):
                ch_ref[i * FINE + j] = 0.5 * (up + down)
                sh_ref[i * FINE + j] = 0.5 * (up - down)
                if i < COARSE - 1:
                    up, down = up * up2, down * down2
            g_ref[j] = jnp.exp(curve * (((2 * j + 1) / 1024.0) ** 2))
        for i in range(COARSE):
            g_ref[FINE + i] = jnp.exp(curve * (((2 * i + 1) / 32.0) ** 2))

        def newton(_, lam):
            mu = lam + curve
            up, down = jnp.exp(mu * (1 / 1024.0)), jnp.exp(mu * (-1 / 1024.0))
            up2, down2 = up * up, down * down
            sums = [[None] * 4 for _ in range(COARSE)]
            for j in range(FINE):
                g = g_ref[j]
                even, odd = g * (up + down), g * (up - down)
                d = (2 * j + 1) / 1024.0
                d_even, d_odd = even * d, odd * d
                for i in range(COARSE):
                    ch, sh = ch_ref[i * FINE + j], sh_ref[i * FINE + j]
                    terms = (ch * even, sh * odd, ch * d_odd, sh * d_even)
                    sums[i] = [t if s is None else s + t for s, t in zip(sums[i], terms)]
                if j < FINE - 1:
                    up, down = up * up2, down * down2
            up, down = jnp.exp(mu * (1 / 32.0)), jnp.exp(mu * (-1 / 32.0))
            up2, down2 = up * up, down * down
            partition, moment = 0.0, 0.0
            for i in range(COARSE):
                g = g_ref[FINE + i]
                even, odd = g * (up + down), g * (up - down)
                a = (2 * i + 1) / 32.0
                e0, o0, o1, e1 = sums[i]
                partition = partition + (even * e0 + odd * o0)
                moment = moment + (a * (odd * e0 + even * o0) + (even * o1 + odd * e1))
                if i < COARSE - 1:
                    up, down = up * up2, down * down2
            return lam + (mean - (0.5 + moment / partition)) * inverse

        lam_ref[chunk, rows, :] = lax.fori_loop(0, ITERS, newton, slope_ref[chunk, 0, rows, :])
        return 0

    lax.fori_loop(0, CHUNKS * per_chunk, body, 0)


def newton(x, slope, curve, mean, var):
    rows = slope.shape[2]
    mine = pl.BlockSpec((CHUNKS, 1, rows, LANES), lambda g, x: (0, x[0], 0, 0))
    return pl.pallas_call(
        newton_kernel,
        out_shape=jax.ShapeDtypeStruct((CHUNKS, rows, LANES), jnp.float32),
        grid_spec=pltpu.PrefetchScalarGridSpec(
            num_scalar_prefetch=1,
            grid=(1,),
            in_specs=[mine] * 4,
            out_specs=pl.BlockSpec((CHUNKS, rows, LANES), lambda g, x: (0, 0, 0)),
            scratch_shapes=[
                pltpu.VMEM((COARSE * FINE, 8, LANES), jnp.float32),
                pltpu.VMEM((COARSE * FINE, 8, LANES), jnp.float32),
                pltpu.VMEM((COARSE + FINE, 8, LANES), jnp.float32),
            ],
        ),
        cost_estimate=pl.CostEstimate(flops=12 * 10**9, bytes_accessed=1 << 18, transcendentals=0),
        name="newton",
    )(x, slope, curve, mean, var)


def species_kernel(x_ref, lam_ref, curve_ref, table_ref, out_ref, turned_ref):
    turned_ref[...] = jnp.transpose(table_ref[...])
    table = jnp.concatenate([turned_ref[pl.ds(p, 8, stride=16), :] for p in range(16)], axis=1)
    high = table.astype(jnp.bfloat16).astype(jnp.float32)
    ones = jnp.ones((16, table.shape[1]), jnp.float32)
    left = jnp.concatenate([high, table - high, ones], axis=0).astype(jnp.bfloat16)
    sub = lax.broadcasted_iota(jnp.int32, (8, LANES), 0).astype(jnp.float32)

    def tile(row):
        lam = jnp.broadcast_to(lam_ref[0, pl.ds(row, 1), :], (8, LANES))
        curve = jnp.broadcast_to(curve_ref[0, 0, pl.ds(row, 1), :], (8, LANES))
        mu = lam + curve
        ratio2 = jnp.exp(curve * (2.0 / (512.0 * 512.0)))
        columns = []
        for g in range(4):
            s = ((sub + 8.0 * g) * 16.0 + 0.5) * (1 / 512.0) - 0.5
            e = jnp.exp(mu * s + curve * (s * s))
            ratio = jnp.exp(mu * (1 / 512.0) + curve * ((2.0 * s + 1 / 512.0) * (1 / 512.0)))
            column = []
            for p in range(16):
                column.append(e)
                if p < 15:
                    e = e * ratio
                    ratio = ratio * ratio2
            columns.append(column)
        return jnp.concatenate([columns[g][p] for p in range(16) for g in range(4)], axis=0)

    def pair(row):
        e = jnp.concatenate([tile(row), tile(row + 1)], axis=1)
        e_high = e.astype(jnp.bfloat16)
        e_low = (e - e_high.astype(jnp.float32)).astype(jnp.bfloat16)
        sums = jnp.dot(left, e_high, preferred_element_type=jnp.float32)
        sums = sums + jnp.dot(left, e_low, preferred_element_type=jnp.float32)
        values = (sums[0:8] + sums[8:16]) / sums[16:24]
        return [values[:, :LANES], values[:, LANES:]]

    def body(t, _):
        values = pair(4 * t) + pair(4 * t + 2)
        rows = pl.ds(pl.multiple_of(8 * t, 8), 8)
        for x in range(4):
            out_ref[x, rows, :] = jnp.concatenate([v[2 * x : 2 * x + 2] for v in values], axis=0)
        return 0

    rows = lam_ref.shape[1]
    lax.fori_loop(0, rows // 4, body, 0)
    for x in range(4):
        out_ref[x, 2 * rows :, :] = lam_ref[0]


def species(x, lam, curve, table):
    rows = lam.shape[1]
    return pl.pallas_call(
        species_kernel,
        out_shape=jax.ShapeDtypeStruct((4, 3 * rows, LANES), jnp.float32),
        grid_spec=pltpu.PrefetchScalarGridSpec(
            num_scalar_prefetch=1,
            grid=(1,),
            in_specs=[
                pl.BlockSpec((1, rows, LANES), lambda g, x: (0, 0, 0)),
                pl.BlockSpec((1, 1, rows, LANES), lambda g, x: (0, x[0], 0, 0)),
                pl.BlockSpec((32, LANES), lambda g, x: (0, 0)),
            ],
            out_specs=pl.BlockSpec((4, 3 * rows, LANES), lambda g, x: (0, 0, 0)),
            scratch_shapes=[pltpu.VMEM((LANES, 32), jnp.float32)],
        ),
        cost_estimate=pl.CostEstimate(flops=6 * 10**9, bytes_accessed=1 << 19, transcendentals=0),
        name="species",
    )(x, lam, curve, table)


def lay_kernel(core_ref, own_ref, other_ref, species_ref, lam_ref, sems):
    rows = lam_ref.shape[3]
    copies = []
    for flip, blocks in ((0, own_ref), (1, other_ref)):
        core = core_ref[0] ^ flip
        for y in range(4):
            copies.append((blocks.at[y, :, pl.ds(0, 2 * rows), :], species_ref.at[y, core]))
            copies.append((blocks.at[y, :, pl.ds(2 * rows, rows), :], lam_ref.at[y, core]))
    started = [pltpu.make_async_copy(a, b, sems.at[i]) for i, (a, b) in enumerate(copies)]
    for copy in started:
        copy.start()
    for copy in started:
        copy.wait()


def lay(core, own, other):
    anywhere = pl.BlockSpec(memory_space=pl.ANY)
    rows = own.shape[2] // 3
    return pl.pallas_call(
        lay_kernel,
        out_shape=[
            jax.ShapeDtypeStruct((4, 2, 4, 2 * rows, LANES), jnp.float32),
            jax.ShapeDtypeStruct((4, 2, 4, rows, LANES), jnp.float32),
        ],
        in_specs=[pl.BlockSpec(memory_space=pltpu.SMEM), anywhere, anywhere],
        out_specs=[anywhere] * 2,
        scratch_shapes=[pltpu.SemaphoreType.DMA((16,))],
        name="lay",
    )(core, own, other)


def exchange(array, axes):
    return lax.all_to_all(array, axes, split_axis=0, concat_axis=0, tiled=True)


def per_device(slope, curvature, target_mean, target_var, table):
    x = jnp.reshape(lax.axis_index("x"), (1,)).astype(jnp.int32)
    core = jnp.reshape(lax.axis_index("core"), (1,)).astype(jnp.int32)
    sent = jnp.broadcast_to(table.reshape(8, 1, 8 * 16), (8, 4, 8 * 16)).reshape(32, 8 * 16)
    points = exchange(sent, ("z", "x"))

    bins = slope.shape[0]
    rows = bins // (4 * LANES)
    args = [a.reshape(1, 4, rows, LANES) for a in (slope, curvature, target_mean, target_var)]
    lam = newton(x, *args)
    sent = species(x, lam, args[1], points)
    ring = exchange(sent, "x")
    own = exchange(jnp.broadcast_to(ring[None], (4, *ring.shape)), "y")
    other = lax.ppermute(own, "core", [(0, 1), (1, 0)])
    values, final_slope = lay(core, own, other)
    values = jnp.transpose(values.reshape(-1, 2, LANES), (1, 0, 2)).reshape(2, -1)
    return values, final_slope.reshape(-1)


def solution(mesh):
    mesh = jax.sharding.Mesh(np.reshape(mesh.devices, (8, 4, 4, 2)), ("z", "x", "y", "core"))
    bins = P(("y", "core"))
    placed = (bins, bins, bins, bins, P(None, ("z", "x")))
    return jax.shard_map(
        per_device, mesh=mesh, in_specs=placed, out_specs=(P(("z", "x"), None), P()), check_vma=False
    )
```

```python
import jax
import jax.numpy as jnp
import numpy as np
from jax import lax
from jax.experimental import pallas as pl
from jax.experimental.pallas import tpu as pltpu
from jax.sharding import PartitionSpec as P

ITERS = 3
CHUNKS = 1
PIECES = 2
LANES = 128
COARSE = 8
FINE = 16


def newton_kernel(x_ref, slope_ref, curve_ref, mean_ref, var_ref, lam_ref, ch_ref, sh_ref, g_ref):
    per_chunk = lam_ref.shape[1] // 8

    def body(v, _):
        chunk = v // per_chunk
        rows = pl.ds(pl.multiple_of((v % per_chunk) * 8, 8), 8)
        curve = curve_ref[chunk, 0, rows, :]
        mean = mean_ref[chunk, 0, rows, :]
        inverse = 1.0 / var_ref[chunk, 0, rows, :]
        for j in range(FINE):
            angle = curve * ((2 * j + 1) / 16384.0)
            up, down = jnp.exp(angle), jnp.exp(-angle)
            up2, down2 = up * up, down * down
            for i in range(COARSE):
                ch_ref[i * FINE + j] = 0.5 * (up + down)
                sh_ref[i * FINE + j] = 0.5 * (up - down)
                if i < COARSE - 1:
                    up, down = up * up2, down * down2
            g_ref[j] = jnp.exp(curve * (((2 * j + 1) / 1024.0) ** 2))
        for i in range(COARSE):
            g_ref[FINE + i] = jnp.exp(curve * (((2 * i + 1) / 32.0) ** 2))

        def newton(_, lam):
            mu = lam + curve
            up, down = jnp.exp(mu * (1 / 1024.0)), jnp.exp(mu * (-1 / 1024.0))
            up2, down2 = up * up, down * down
            sums = [[None] * 4 for _ in range(COARSE)]
            for j in range(FINE):
                g = g_ref[j]
                even, odd = g * (up + down), g * (up - down)
                d = (2 * j + 1) / 1024.0
                d_even, d_odd = even * d, odd * d
                for i in range(COARSE):
                    ch, sh = ch_ref[i * FINE + j], sh_ref[i * FINE + j]
                    terms = (ch * even, sh * odd, ch * d_odd, sh * d_even)
                    sums[i] = [t if s is None else s + t for s, t in zip(sums[i], terms)]
                if j < FINE - 1:
                    up, down = up * up2, down * down2
            up, down = jnp.exp(mu * (1 / 32.0)), jnp.exp(mu * (-1 / 32.0))
            up2, down2 = up * up, down * down
            partition, moment = 0.0, 0.0
            for i in range(COARSE):
                g = g_ref[FINE + i]
                even, odd = g * (up + down), g * (up - down)
                a = (2 * i + 1) / 32.0
                e0, o0, o1, e1 = sums[i]
                partition = partition + (even * e0 + odd * o0)
                moment = moment + (a * (odd * e0 + even * o0) + (even * o1 + odd * e1))
                if i < COARSE - 1:
                    up, down = up * up2, down * down2
            return lam + (mean - (0.5 + moment / partition)) * inverse

        lam_ref[chunk, rows, :] = lax.fori_loop(0, ITERS, newton, slope_ref[chunk, 0, rows, :])
        return 0

    lax.fori_loop(0, CHUNKS * per_chunk, body, 0)


def newton(x, slope, curve, mean, var):
    rows = slope.shape[2]
    mine = pl.BlockSpec((CHUNKS, 1, rows, LANES), lambda g, x: (0, x[0], 0, 0))
    return pl.pallas_call(
        newton_kernel,
        out_shape=jax.ShapeDtypeStruct((CHUNKS, rows, LANES), jnp.float32),
        grid_spec=pltpu.PrefetchScalarGridSpec(
            num_scalar_prefetch=1,
            grid=(1,),
            in_specs=[mine] * 4,
            out_specs=pl.BlockSpec((CHUNKS, rows, LANES), lambda g, x: (0, 0, 0)),
            scratch_shapes=[
                pltpu.VMEM((COARSE * FINE, 8, LANES), jnp.float32),
                pltpu.VMEM((COARSE * FINE, 8, LANES), jnp.float32),
                pltpu.VMEM((COARSE + FINE, 8, LANES), jnp.float32),
            ],
        ),
        cost_estimate=pl.CostEstimate(flops=12 * 10**9, bytes_accessed=1 << 18, transcendentals=0),
        name="newton",
    )(x, slope, curve, mean, var)


def species_kernel(x_ref, lam_ref, curve_ref, table_ref, out_ref, turned_ref):
    turned_ref[...] = jnp.transpose(table_ref[...])
    table = jnp.concatenate([turned_ref[pl.ds(p, 8, stride=16), :] for p in range(16)], axis=1)
    high = table.astype(jnp.bfloat16).astype(jnp.float32)
    ones = jnp.ones((16, table.shape[1]), jnp.float32)
    left = jnp.concatenate([high, table - high, ones], axis=0).astype(jnp.bfloat16)
    sub = lax.broadcasted_iota(jnp.int32, (8, LANES), 0).astype(jnp.float32)

    def tile(row):
        lam = jnp.broadcast_to(lam_ref[0, pl.ds(row, 1), :], (8, LANES))
        curve = jnp.broadcast_to(curve_ref[0, 0, pl.ds(row, 1), :], (8, LANES))
        mu = lam + curve
        ratio2 = jnp.exp(curve * (2.0 / (512.0 * 512.0)))
        columns = []
        for g in range(4):
            s = ((sub + 8.0 * g) * 16.0 + 0.5) * (1 / 512.0) - 0.5
            e = jnp.exp(mu * s + curve * (s * s))
            ratio = jnp.exp(mu * (1 / 512.0) + curve * ((2.0 * s + 1 / 512.0) * (1 / 512.0)))
            column = []
            for p in range(16):
                column.append(e)
                if p < 15:
                    e = e * ratio
                    ratio = ratio * ratio2
            columns.append(column)
        return jnp.concatenate([columns[g][p] for p in range(16) for g in range(4)], axis=0)

    def pair(row):
        e = jnp.concatenate([tile(row), tile(row + 1)], axis=1)
        e_high = e.astype(jnp.bfloat16)
        e_low = (e - e_high.astype(jnp.float32)).astype(jnp.bfloat16)
        sums = jnp.dot(left, e_high, preferred_element_type=jnp.float32)
        sums = sums + jnp.dot(left, e_low, preferred_element_type=jnp.float32)
        values = (sums[0:8] + sums[8:16]) / sums[16:24]
        return [values[:, :LANES], values[:, LANES:]]

    def body(t, _):
        values = pair(4 * t) + pair(4 * t + 2)
        rows = pl.ds(pl.multiple_of(8 * t, 8), 8)
        for x in range(4):
            out_ref[x, rows, :] = jnp.concatenate([v[2 * x : 2 * x + 2] for v in values], axis=0)
        return 0

    lax.fori_loop(0, lam_ref.shape[1] // 4, body, 0)


def species(x, lam, curve, table, piece):
    rows = lam.shape[1] // PIECES
    return pl.pallas_call(
        species_kernel,
        out_shape=jax.ShapeDtypeStruct((4, 2 * rows, LANES), jnp.float32),
        grid_spec=pltpu.PrefetchScalarGridSpec(
            num_scalar_prefetch=1,
            grid=(1,),
            in_specs=[
                pl.BlockSpec((1, rows, LANES), lambda g, x: (0, piece, 0)),
                pl.BlockSpec((1, 1, rows, LANES), lambda g, x: (0, x[0], piece, 0)),
                pl.BlockSpec((32, LANES), lambda g, x: (0, 0)),
            ],
            out_specs=pl.BlockSpec((4, 2 * rows, LANES), lambda g, x: (0, 0, 0)),
            scratch_shapes=[pltpu.VMEM((LANES, 32), jnp.float32)],
        ),
        cost_estimate=pl.CostEstimate(
            flops=12 * 10**9 // PIECES, bytes_accessed=1 << 19, transcendentals=0
        ),
        name="species",
    )(x, lam, curve, table)


def lay_kernel(core_ref, *refs):
    blocks, (out_ref, sems) = refs[:-2], refs[-2:]
    started = []
    for n, block in enumerate(blocks):
        piece, core = n // 2, core_ref[0] ^ (n % 2)
        for y in range(4):
            copy = pltpu.make_async_copy(
                block.at[:, y], out_ref.at[y, core, :, piece], sems.at[4 * n + y]
            )
            copy.start()
            started.append(copy)
    for copy in started:
        copy.wait()


def lay(core, *blocks):
    rows = blocks[0].shape[2]
    return pl.pallas_call(
        lay_kernel,
        out_shape=jax.ShapeDtypeStruct((4, 2, 4, len(blocks) // 2, rows, LANES), jnp.float32),
        in_specs=[pl.BlockSpec(memory_space=pltpu.SMEM)]
        + [pl.BlockSpec(memory_space=pltpu.VMEM)] * len(blocks),
        out_specs=pl.BlockSpec(memory_space=pl.ANY),
        scratch_shapes=[pltpu.SemaphoreType.DMA((4 * len(blocks),))],
        cost_estimate=pl.CostEstimate(flops=2 * 10**9, bytes_accessed=1 << 21, transcendentals=0),
        name="lay",
    )(core, *blocks)


def exchange(array, axes):
    return lax.all_to_all(array, axes, split_axis=0, concat_axis=0, tiled=True)


def gather(block, per_x=False):
    block = block[:, None] if per_x else block[None, None]
    own = exchange(jnp.broadcast_to(block, (4, 4, *block.shape[2:])).reshape(16, *block.shape[2:]), ("x", "y"))
    own = own.reshape(4, 4, *block.shape[2:])
    return [own, lax.ppermute(own, "core", [(0, 1), (1, 0)])]


def per_device(slope, curvature, target_mean, target_var, table):
    x = jnp.reshape(lax.axis_index("x"), (1,)).astype(jnp.int32)
    core = jnp.reshape(lax.axis_index("core"), (1,)).astype(jnp.int32)
    sent = jnp.broadcast_to(table.reshape(8, 1, 8 * 16), (8, 4, 8 * 16)).reshape(32, 8 * 16)
    points = exchange(sent, ("z", "x"))

    bins = slope.shape[0]
    rows = bins // (4 * LANES)
    args = [a.reshape(1, 4, rows, LANES) for a in (slope, curvature, target_mean, target_var)]
    lam = newton(x, *args)
    lam_blocks = gather(lam[0])
    pieces = []
    for piece in range(PIECES):
        pieces += gather(species(x, lam, args[1], points, piece), per_x=True)
    values, final_slope = lay(core, *pieces), lay(core, *lam_blocks)
    values = jnp.transpose(values.reshape(-1, 2, LANES), (1, 0, 2)).reshape(2, -1)
    return values, final_slope.reshape(-1)


def solution(mesh):
    mesh = jax.sharding.Mesh(np.reshape(mesh.devices, (8, 4, 4, 2)), ("z", "x", "y", "core"))
    bins = P(("y", "core"))
    placed = (bins, bins, bins, bins, P(None, ("z", "x")))
    return jax.shard_map(
        per_device, mesh=mesh, in_specs=placed, out_specs=(P(("z", "x"), None), P()), check_vma=False
    )
```

```python
import functools

import jax
import jax.numpy as jnp
import numpy as np
from jax import lax
from jax.experimental import pallas as pl
from jax.experimental.pallas import tpu as pltpu
from jax.sharding import PartitionSpec as P

ITERS = 3
CHUNKS = 1
LANES = 128
COARSE = 8
FINE = 16


def newton_kernel(x_ref, slope_ref, curve_ref, mean_ref, var_ref, lam_ref, ch_ref, sh_ref, g_ref):
    per_chunk = lam_ref.shape[1] // 8

    def body(v, _):
        chunk = v // per_chunk
        rows = pl.ds(pl.multiple_of((v % per_chunk) * 8, 8), 8)
        curve = curve_ref[chunk, 0, rows, :]
        mean = mean_ref[chunk, 0, rows, :]
        inverse = 1.0 / var_ref[chunk, 0, rows, :]
        for j in range(FINE):
            angle = curve * ((2 * j + 1) / 16384.0)
            up, down = jnp.exp(angle), jnp.exp(-angle)
            up2, down2 = up * up, down * down
            for i in range(COARSE):
                ch_ref[i * FINE + j] = 0.5 * (up + down)
                sh_ref[i * FINE + j] = 0.5 * (up - down)
                if i < COARSE - 1:
                    up, down = up * up2, down * down2
            g_ref[j] = jnp.exp(curve * (((2 * j + 1) / 1024.0) ** 2))
        for i in range(COARSE):
            g_ref[FINE + i] = jnp.exp(curve * (((2 * i + 1) / 32.0) ** 2))

        def newton(_, lam):
            mu = lam + curve
            up, down = jnp.exp(mu * (1 / 1024.0)), jnp.exp(mu * (-1 / 1024.0))
            up2, down2 = up * up, down * down
            sums = [[None] * 4 for _ in range(COARSE)]
            for j in range(FINE):
                g = g_ref[j]
                even, odd = g * (up + down), g * (up - down)
                d = (2 * j + 1) / 1024.0
                d_even, d_odd = even * d, odd * d
                for i in range(COARSE):
                    ch, sh = ch_ref[i * FINE + j], sh_ref[i * FINE + j]
                    terms = (ch * even, sh * odd, ch * d_odd, sh * d_even)
                    sums[i] = [t if s is None else s + t for s, t in zip(sums[i], terms)]
                if j < FINE - 1:
                    up, down = up * up2, down * down2
            up, down = jnp.exp(mu * (1 / 32.0)), jnp.exp(mu * (-1 / 32.0))
            up2, down2 = up * up, down * down
            partition, moment = 0.0, 0.0
            for i in range(COARSE):
                g = g_ref[FINE + i]
                even, odd = g * (up + down), g * (up - down)
                a = (2 * i + 1) / 32.0
                e0, o0, o1, e1 = sums[i]
                partition = partition + (even * e0 + odd * o0)
                moment = moment + (a * (odd * e0 + even * o0) + (even * o1 + odd * e1))
                if i < COARSE - 1:
                    up, down = up * up2, down * down2
            return lam + (mean - (0.5 + moment / partition)) * inverse

        lam_ref[chunk, rows, :] = lax.fori_loop(0, ITERS, newton, slope_ref[chunk, 0, rows, :])
        return 0

    lax.fori_loop(0, CHUNKS * per_chunk, body, 0)


def newton(x, slope, curve, mean, var):
    rows = slope.shape[2]
    mine = pl.BlockSpec((CHUNKS, 1, rows, LANES), lambda g, x: (0, x[0], 0, 0))
    return pl.pallas_call(
        newton_kernel,
        out_shape=jax.ShapeDtypeStruct((CHUNKS, rows, LANES), jnp.float32),
        grid_spec=pltpu.PrefetchScalarGridSpec(
            num_scalar_prefetch=1,
            grid=(1,),
            in_specs=[mine] * 4,
            out_specs=pl.BlockSpec(memory_space=pltpu.VMEM),
            scratch_shapes=[
                pltpu.VMEM((COARSE * FINE, 8, LANES), jnp.float32),
                pltpu.VMEM((COARSE * FINE, 8, LANES), jnp.float32),
                pltpu.VMEM((COARSE + FINE, 8, LANES), jnp.float32),
            ],
        ),
        cost_estimate=pl.CostEstimate(flops=12 * 10**9, bytes_accessed=1 << 18, transcendentals=0),
        name="newton",
    )(x, slope, curve, mean, var)


def species_kernel(x_ref, lam_ref, curve_ref, table_ref, sent_ref, turned_ref, out_ref, sems):
    turned_ref[...] = jnp.transpose(table_ref[...])
    table = jnp.concatenate([turned_ref[pl.ds(p, 8, stride=16), :] for p in range(16)], axis=1)
    high = table.astype(jnp.bfloat16).astype(jnp.float32)
    ones = jnp.ones((16, table.shape[1]), jnp.float32)
    left = jnp.concatenate([high, table - high, ones], axis=0).astype(jnp.bfloat16)
    sub = lax.broadcasted_iota(jnp.int32, (8, LANES), 0).astype(jnp.float32)

    def tile(row):
        lam = jnp.broadcast_to(lam_ref[0, pl.ds(row, 1), :], (8, LANES))
        curve = jnp.broadcast_to(curve_ref[0, 0, pl.ds(row, 1), :], (8, LANES))
        mu = lam + curve
        ratio2 = jnp.exp(curve * (2.0 / (512.0 * 512.0)))
        columns = []
        for g in range(4):
            s = ((sub + 8.0 * g) * 16.0 + 0.5) * (1 / 512.0) - 0.5
            e = jnp.exp(mu * s + curve * (s * s))
            ratio = jnp.exp(mu * (1 / 512.0) + curve * ((2.0 * s + 1 / 512.0) * (1 / 512.0)))
            column = []
            for p in range(16):
                column.append(e)
                if p < 15:
                    e = e * ratio
                    ratio = ratio * ratio2
            columns.append(column)
        return jnp.concatenate([columns[g][p] for p in range(16) for g in range(4)], axis=0)

    def pair(row):
        e = jnp.concatenate([tile(row), tile(row + 1)], axis=1)
        e_high = e.astype(jnp.bfloat16)
        e_low = (e - e_high.astype(jnp.float32)).astype(jnp.bfloat16)
        sums = jnp.dot(left, e_high, preferred_element_type=jnp.float32)
        sums = sums + jnp.dot(left, e_low, preferred_element_type=jnp.float32)
        values = (sums[0:8] + sums[8:16]) / sums[16:24]
        return [values[:, :LANES], values[:, LANES:]]

    def body(t, _):
        values = pair(4 * t) + pair(4 * t + 2)
        rows = pl.ds(pl.multiple_of(8 * t, 8), 8)
        for x in range(4):
            out_ref[x, rows, :] = jnp.concatenate([v[2 * x : 2 * x + 2] for v in values], axis=0)
        return 0

    rows = lam_ref.shape[1]
    for x in range(4):
        out_ref[x, 2 * rows :, :] = lam_ref[0]
    lax.fori_loop(0, rows // 4, body, 0)
    copies = [pltpu.make_async_copy(out_ref, sent_ref.at[:, y], sems.at[y]) for y in range(4)]
    for copy in copies:
        copy.start()
    for copy in copies:
        copy.wait()


def species(x, lam, curve, table):
    rows = lam.shape[1]
    return pl.pallas_call(
        species_kernel,
        out_shape=jax.ShapeDtypeStruct((4, 4, 3 * rows, LANES), jnp.float32),
        grid_spec=pltpu.PrefetchScalarGridSpec(
            num_scalar_prefetch=1,
            grid=(1,),
            in_specs=[
                pl.BlockSpec(memory_space=pltpu.VMEM),
                pl.BlockSpec((1, 1, rows, LANES), lambda g, x: (0, x[0], 0, 0)),
                pl.BlockSpec(memory_space=pltpu.VMEM),
            ],
            out_specs=pl.BlockSpec(memory_space=pl.ANY),
            scratch_shapes=[
                pltpu.VMEM((LANES, 32), jnp.float32),
                pltpu.VMEM((4, 3 * rows, LANES), jnp.float32),
                pltpu.SemaphoreType.DMA((4,)),
            ],
        ),
        cost_estimate=pl.CostEstimate(flops=6 * 10**9, bytes_accessed=1 << 19, transcendentals=0),
        compiler_params=pltpu.CompilerParams(vmem_limit_bytes=16 << 20),
        name="species",
    )(x, lam, curve, table)


def lay_kernel(flip, core_ref, blocks_ref, *refs):
    species_ref, lam_ref, sems = refs[-3:]
    rows = lam_ref.shape[3]
    core = core_ref[0] ^ flip
    copies = []
    for y in range(4):
        copies.append((blocks_ref.at[:, y, pl.ds(0, 2 * rows), :], species_ref.at[y, core]))
        copies.append((blocks_ref.at[:, y, pl.ds(2 * rows, rows), :], lam_ref.at[y, core]))
    started = [pltpu.make_async_copy(a, b, sems.at[i]) for i, (a, b) in enumerate(copies)]
    for copy in started:
        copy.start()
    for copy in started:
        copy.wait()


def lay(core, blocks, flip, laid=()):
    anywhere = pl.BlockSpec(memory_space=pl.ANY)
    rows = blocks.shape[2] // 3
    return pl.pallas_call(
        functools.partial(lay_kernel, flip),
        out_shape=[
            jax.ShapeDtypeStruct((4, 2, 4, 2 * rows, LANES), jnp.float32),
            jax.ShapeDtypeStruct((4, 2, 4, rows, LANES), jnp.float32),
        ],
        in_specs=[pl.BlockSpec(memory_space=pltpu.SMEM), pl.BlockSpec(memory_space=pltpu.VMEM)]
        + [anywhere] * len(laid),
        out_specs=[anywhere] * 2,
        input_output_aliases={2: 0, 3: 1} if laid else {},
        scratch_shapes=[pltpu.SemaphoreType.DMA((8,))],
        cost_estimate=pl.CostEstimate(flops=2 * 10**9, bytes_accessed=3 << 20, transcendentals=0),
        compiler_params=pltpu.CompilerParams(vmem_limit_bytes=4 << 20),
        name="lay",
    )(core, blocks, *laid)


def exchange(array, axes):
    return lax.all_to_all(array, axes, split_axis=0, concat_axis=0, tiled=True)


def per_device(slope, curvature, target_mean, target_var, table):
    x = jnp.reshape(lax.axis_index("x"), (1,)).astype(jnp.int32)
    core = jnp.reshape(lax.axis_index("core"), (1,)).astype(jnp.int32)
    sent = jnp.broadcast_to(table.reshape(8, 1, 8 * 16), (8, 4, 8 * 16)).reshape(32, 8 * 16)
    points = exchange(sent, ("z", "x"))

    bins = slope.shape[0]
    rows = bins // (4 * LANES)
    args = [a.reshape(1, 4, rows, LANES) for a in (slope, curvature, target_mean, target_var)]
    lam = newton(x, *args)
    sent = species(x, lam, args[1], points)
    own = exchange(sent.reshape(16, *sent.shape[2:]), ("x", "y")).reshape(sent.shape)
    other = lax.ppermute(own, "core", [(0, 1), (1, 0)])
    values, final_slope = lay(core, other, 1, lay(core, own, 0))
    values = jnp.transpose(values.reshape(-1, 2, LANES), (1, 0, 2)).reshape(2, -1)
    return values, final_slope.reshape(-1)


def solution(mesh):
    mesh = jax.sharding.Mesh(np.reshape(mesh.devices, (8, 4, 4, 2)), ("z", "x", "y", "core"))
    bins = P(("y", "core"))
    placed = (bins, bins, bins, bins, P(None, ("z", "x")))
    return jax.shard_map(
        per_device, mesh=mesh, in_specs=placed, out_specs=(P(("z", "x"), None), P()), check_vma=False
    )
```

```python
import functools

import jax
import jax.numpy as jnp
import numpy as np
from jax import lax
from jax.experimental import pallas as pl
from jax.experimental.pallas import tpu as pltpu
from jax.sharding import PartitionSpec as P

ITERS = 3
LANES = 128
COARSE = 8
FINE = 16


def newton_kernel(x_ref, *refs):
    whole, (lam_ref, curve_ref, slope_ref, mean_ref, var_ref) = refs[:4], refs[4:9]
    ch_ref, sh_ref, g_ref, sems = refs[9:]
    mine = zip(whole, (slope_ref, curve_ref, mean_ref, var_ref))
    copies = [pltpu.make_async_copy(a.at[x_ref[0]], b, sems.at[i]) for i, (a, b) in enumerate(mine)]
    for copy in copies:
        copy.start()
    for copy in copies:
        copy.wait()

    def body(v, _):
        rows = pl.ds(pl.multiple_of(v * 8, 8), 8)
        curve = curve_ref[rows, :]
        mean = mean_ref[rows, :]
        inverse = 1.0 / var_ref[rows, :]
        for j in range(FINE):
            angle = curve * ((2 * j + 1) / 16384.0)
            up, down = jnp.exp(angle), jnp.exp(-angle)
            up2, down2 = up * up, down * down
            for i in range(COARSE):
                ch_ref[i * FINE + j] = 0.5 * (up + down)
                sh_ref[i * FINE + j] = 0.5 * (up - down)
                if i < COARSE - 1:
                    up, down = up * up2, down * down2
            g_ref[j] = jnp.exp(curve * (((2 * j + 1) / 1024.0) ** 2))
        for i in range(COARSE):
            g_ref[FINE + i] = jnp.exp(curve * (((2 * i + 1) / 32.0) ** 2))

        def newton(_, lam):
            mu = lam + curve
            up, down = jnp.exp(mu * (1 / 1024.0)), jnp.exp(mu * (-1 / 1024.0))
            up2, down2 = up * up, down * down
            sums = [[None] * 4 for _ in range(COARSE)]
            for j in range(FINE):
                g = g_ref[j]
                even, odd = g * (up + down), g * (up - down)
                d = (2 * j + 1) / 1024.0
                d_even, d_odd = even * d, odd * d
                for i in range(COARSE):
                    ch, sh = ch_ref[i * FINE + j], sh_ref[i * FINE + j]
                    terms = (ch * even, sh * odd, ch * d_odd, sh * d_even)
                    sums[i] = [t if s is None else s + t for s, t in zip(sums[i], terms)]
                if j < FINE - 1:
                    up, down = up * up2, down * down2
            up, down = jnp.exp(mu * (1 / 32.0)), jnp.exp(mu * (-1 / 32.0))
            up2, down2 = up * up, down * down
            partition, moment = 0.0, 0.0
            for i in range(COARSE):
                g = g_ref[FINE + i]
                even, odd = g * (up + down), g * (up - down)
                a = (2 * i + 1) / 32.0
                e0, o0, o1, e1 = sums[i]
                partition = partition + (even * e0 + odd * o0)
                moment = moment + (a * (odd * e0 + even * o0) + (even * o1 + odd * e1))
                if i < COARSE - 1:
                    up, down = up * up2, down * down2
            return lam + (mean - (0.5 + moment / partition)) * inverse

        lam_ref[rows, :] = lax.fori_loop(0, ITERS, newton, slope_ref[rows, :])
        return 0

    lax.fori_loop(0, lam_ref.shape[0] // 8, body, 0)


def newton(x, slope, curve, mean, var):
    rows = slope.shape[1]
    part = jax.ShapeDtypeStruct((rows, LANES), jnp.float32)
    return pl.pallas_call(
        newton_kernel,
        out_shape=[part, part],
        in_specs=[pl.BlockSpec(memory_space=pltpu.SMEM)] + [pl.BlockSpec(memory_space=pltpu.HBM)] * 4,
        out_specs=[pl.BlockSpec(memory_space=pltpu.VMEM)] * 2,
        scratch_shapes=[pltpu.VMEM((rows, LANES), jnp.float32)] * 3
        + [pltpu.VMEM((COARSE * FINE, 8, LANES), jnp.float32)] * 2
        + [pltpu.VMEM((COARSE + FINE, 8, LANES), jnp.float32), pltpu.SemaphoreType.DMA((4,))],
        cost_estimate=pl.CostEstimate(flops=12 * 10**9, bytes_accessed=1 << 18, transcendentals=0),
        compiler_params=pltpu.CompilerParams(vmem_limit_bytes=8 << 20),
        name="newton",
    )(x, slope, curve, mean, var)


def species_kernel(lam_ref, curve_ref, table_ref, sent_ref, turned_ref):
    turned_ref[...] = jnp.transpose(table_ref[...])
    table = jnp.concatenate([turned_ref[pl.ds(p, 8, stride=16), :] for p in range(16)], axis=1)
    high = table.astype(jnp.bfloat16).astype(jnp.float32)
    ones = jnp.ones((16, table.shape[1]), jnp.float32)
    left = jnp.concatenate([high, table - high, ones], axis=0).astype(jnp.bfloat16)
    sub = lax.broadcasted_iota(jnp.int32, (8, LANES), 0).astype(jnp.float32)

    def tile(row):
        lam = jnp.broadcast_to(lam_ref[pl.ds(row, 1), :], (8, LANES))
        curve = jnp.broadcast_to(curve_ref[pl.ds(row, 1), :], (8, LANES))
        mu = lam + curve
        ratio2 = jnp.exp(curve * (2.0 / (512.0 * 512.0)))
        columns = []
        for g in range(4):
            s = ((sub + 8.0 * g) * 16.0 + 0.5) * (1 / 512.0) - 0.5
            e = jnp.exp(mu * s + curve * (s * s))
            ratio = jnp.exp(mu * (1 / 512.0) + curve * ((2.0 * s + 1 / 512.0) * (1 / 512.0)))
            column = []
            for p in range(16):
                column.append(e)
                if p < 15:
                    e = e * ratio
                    ratio = ratio * ratio2
            columns.append(column)
        return jnp.concatenate([columns[g][p] for p in range(16) for g in range(4)], axis=0)

    def pair(row):
        e = jnp.concatenate([tile(row), tile(row + 1)], axis=1)
        e_high = e.astype(jnp.bfloat16)
        e_low = (e - e_high.astype(jnp.float32)).astype(jnp.bfloat16)
        sums = jnp.dot(left, e_high, preferred_element_type=jnp.float32)
        sums = sums + jnp.dot(left, e_low, preferred_element_type=jnp.float32)
        values = (sums[0:8] + sums[8:16]) / sums[16:24]
        return [values[:, :LANES], values[:, LANES:]]

    def body(t, _):
        values = pair(4 * t) + pair(4 * t + 2)
        rows = pl.ds(pl.multiple_of(8 * t, 8), 8)
        for x in range(4):
            block = jnp.concatenate([v[2 * x : 2 * x + 2] for v in values], axis=0)
            for y in range(4):
                sent_ref[x, y, rows, :] = block
        return 0

    rows = lam_ref.shape[0]
    for x in range(4):
        for y in range(4):
            sent_ref[x, y, 2 * rows :, :] = lam_ref[...]
    lax.fori_loop(0, rows // 4, body, 0, unroll=4)


def species(lam, curve, table):
    rows = lam.shape[0]
    return pl.pallas_call(
        species_kernel,
        out_shape=jax.ShapeDtypeStruct((4, 4, 3 * rows, LANES), jnp.float32),
        in_specs=[pl.BlockSpec(memory_space=pltpu.VMEM)] * 3,
        out_specs=pl.BlockSpec(memory_space=pltpu.VMEM),
        scratch_shapes=[pltpu.VMEM((LANES, 32), jnp.float32)],
        cost_estimate=pl.CostEstimate(flops=6 * 10**9, bytes_accessed=1 << 19, transcendentals=0),
        compiler_params=pltpu.CompilerParams(vmem_limit_bytes=16 << 20),
        name="species",
    )(lam, curve, table)


def blocks_kernel(table_ref, out_ref, turned_ref):
    points = table_ref.shape[0]
    turned_ref[:, :points] = jnp.transpose(table_ref[...])
    block = [turned_ref[pl.ds(q, 8, stride=8), :points] for q in range(8)]
    block = jnp.concatenate(block, axis=1)
    out_ref[...] = jnp.broadcast_to(block[:, None, :], out_ref.shape)


def blocks(table):
    return pl.pallas_call(
        blocks_kernel,
        out_shape=jax.ShapeDtypeStruct((8, 4, LANES), jnp.float32),
        in_specs=[pl.BlockSpec(memory_space=pltpu.VMEM)],
        out_specs=pl.BlockSpec(memory_space=pltpu.VMEM),
        scratch_shapes=[pltpu.VMEM((64, LANES), jnp.float32)],
        compiler_params=pltpu.CompilerParams(vmem_limit_bytes=4 << 20),
        name="blocks",
    )(table)


def lay_kernel(flip, core_ref, blocks_ref, *refs):
    species_ref, lam_ref, sems = refs[-3:]
    rows = lam_ref.shape[3]
    core = core_ref[0] ^ flip
    copies = []
    for y in range(4):
        copies.append((blocks_ref.at[:, y, pl.ds(0, 2 * rows), :], species_ref.at[y, core]))
        copies.append((blocks_ref.at[:, y, pl.ds(2 * rows, rows), :], lam_ref.at[y, core]))
    started = [pltpu.make_async_copy(a, b, sems.at[i]) for i, (a, b) in enumerate(copies)]
    for copy in started:
        copy.start()
    for copy in started:
        copy.wait()


def lay(core, blocks, flip, laid=()):
    anywhere = pl.BlockSpec(memory_space=pl.ANY)
    rows = blocks.shape[2] // 3
    return pl.pallas_call(
        functools.partial(lay_kernel, flip),
        out_shape=[
            jax.ShapeDtypeStruct((4, 2, 4, 2 * rows, LANES), jnp.float32),
            jax.ShapeDtypeStruct((4, 2, 4, rows, LANES), jnp.float32),
        ],
        in_specs=[pl.BlockSpec(memory_space=pltpu.SMEM), pl.BlockSpec(memory_space=pltpu.VMEM)]
        + [anywhere] * len(laid),
        out_specs=[anywhere] * 2,
        input_output_aliases={2: 0, 3: 1} if laid else {},
        scratch_shapes=[pltpu.SemaphoreType.DMA((8,))],
        cost_estimate=pl.CostEstimate(flops=2 * 10**9, bytes_accessed=3 << 20, transcendentals=0),
        compiler_params=pltpu.CompilerParams(vmem_limit_bytes=4 << 20),
        name="lay",
    )(core, blocks, *laid)


def exchange(array, axes):
    return lax.all_to_all(array, axes, split_axis=0, concat_axis=0, tiled=True)


def per_device(slope, curvature, target_mean, target_var, table):
    x = jnp.reshape(lax.axis_index("x"), (1,)).astype(jnp.int32)
    core = jnp.reshape(lax.axis_index("core"), (1,)).astype(jnp.int32)
    points = exchange(blocks(table.T).reshape(32, LANES), ("z", "x"))

    bins = slope.shape[0]
    rows = bins // (4 * LANES)
    args = [a.reshape(4, rows, LANES) for a in (slope, curvature, target_mean, target_var)]
    lam, curve = newton(x, *args)
    sent = species(lam, curve, points)
    own = exchange(sent.reshape(16, *sent.shape[2:]), ("x", "y")).reshape(sent.shape)
    other = lax.ppermute(own, "core", [(0, 1), (1, 0)])
    values, final_slope = lay(core, other, 1, lay(core, own, 0))
    values = jnp.transpose(values.reshape(-1, 2, LANES), (1, 0, 2)).reshape(2, -1)
    return values, final_slope.reshape(-1)


def solution(mesh):
    mesh = jax.sharding.Mesh(np.reshape(mesh.devices, (8, 4, 4, 2)), ("z", "x", "y", "core"))
    bins = P(("y", "core"))
    placed = (bins, bins, bins, bins, P(None, ("z", "x")))
    return jax.shard_map(
        per_device, mesh=mesh, in_specs=placed, out_specs=(P(("z", "x"), None), P()), check_vma=False
    )
```

```python
import functools

import jax
import jax.numpy as jnp
import numpy as np
from jax import lax
from jax.experimental import pallas as pl
from jax.experimental.pallas import tpu as pltpu
from jax.sharding import PartitionSpec as P

ITERS = 3
LANES = 128
COARSE = 8
FINE = 16


def newton_kernel(slope_ref, curve_ref, mean_ref, var_ref, lam_ref, ch_ref, sh_ref, g_ref):
    def body(v, _):
        rows = pl.ds(pl.multiple_of(v * 8, 8), 8)
        curve = curve_ref[rows, :]
        mean = mean_ref[rows, :]
        inverse = 1.0 / var_ref[rows, :]
        for j in range(FINE):
            angle = curve * ((2 * j + 1) / 16384.0)
            up, down = jnp.exp(angle), jnp.exp(-angle)
            up2, down2 = up * up, down * down
            for i in range(COARSE):
                ch_ref[i * FINE + j] = 0.5 * (up + down)
                sh_ref[i * FINE + j] = 0.5 * (up - down)
                if i < COARSE - 1:
                    up, down = up * up2, down * down2
            g_ref[j] = jnp.exp(curve * (((2 * j + 1) / 1024.0) ** 2))
        for i in range(COARSE):
            g_ref[FINE + i] = jnp.exp(curve * (((2 * i + 1) / 32.0) ** 2))

        def newton(_, lam):
            mu = lam + curve
            up, down = jnp.exp(mu * (1 / 1024.0)), jnp.exp(mu * (-1 / 1024.0))
            up2, down2 = up * up, down * down
            sums = [[None] * 4 for _ in range(COARSE)]
            for j in range(FINE):
                g = g_ref[j]
                even, odd = g * (up + down), g * (up - down)
                d = (2 * j + 1) / 1024.0
                d_even, d_odd = even * d, odd * d
                for i in range(COARSE):
                    ch, sh = ch_ref[i * FINE + j], sh_ref[i * FINE + j]
                    terms = (ch * even, sh * odd, ch * d_odd, sh * d_even)
                    sums[i] = [t if s is None else s + t for s, t in zip(sums[i], terms)]
                if j < FINE - 1:
                    up, down = up * up2, down * down2
            up, down = jnp.exp(mu * (1 / 32.0)), jnp.exp(mu * (-1 / 32.0))
            up2, down2 = up * up, down * down
            partition, moment = 0.0, 0.0
            for i in range(COARSE):
                g = g_ref[FINE + i]
                even, odd = g * (up + down), g * (up - down)
                a = (2 * i + 1) / 32.0
                e0, o0, o1, e1 = sums[i]
                partition = partition + (even * e0 + odd * o0)
                moment = moment + (a * (odd * e0 + even * o0) + (even * o1 + odd * e1))
                if i < COARSE - 1:
                    up, down = up * up2, down * down2
            return lam + (mean - (0.5 + moment / partition)) * inverse

        lam_ref[rows, :] = lax.fori_loop(0, ITERS, newton, slope_ref[rows, :])
        return 0

    lax.fori_loop(0, lam_ref.shape[0] // 8, body, 0)


def newton(slope, curve, mean, var):
    return pl.pallas_call(
        newton_kernel,
        out_shape=jax.ShapeDtypeStruct(slope.shape, jnp.float32),
        in_specs=[pl.BlockSpec(memory_space=pltpu.VMEM)] * 4,
        out_specs=pl.BlockSpec(memory_space=pltpu.VMEM),
        scratch_shapes=[pltpu.VMEM((COARSE * FINE, 8, LANES), jnp.float32)] * 2
        + [pltpu.VMEM((COARSE + FINE, 8, LANES), jnp.float32)],
        cost_estimate=pl.CostEstimate(flops=12 * 10**9, bytes_accessed=1 << 18, transcendentals=0),
        compiler_params=pltpu.CompilerParams(vmem_limit_bytes=8 << 20),
        name="newton",
    )(slope, curve, mean, var)


def species_kernel(lam_ref, curve_ref, table_ref, sent_ref, turned_ref):
    turned_ref[...] = jnp.transpose(table_ref[...])
    table = jnp.concatenate([turned_ref[pl.ds(p, 8, stride=16), :] for p in range(16)], axis=1)
    high = table.astype(jnp.bfloat16).astype(jnp.float32)
    ones = jnp.ones((16, table.shape[1]), jnp.float32)
    left = jnp.concatenate([high, table - high, ones], axis=0).astype(jnp.bfloat16)
    sub = lax.broadcasted_iota(jnp.int32, (8, LANES), 0).astype(jnp.float32)

    def tile(row):
        lam = jnp.broadcast_to(lam_ref[pl.ds(row, 1), :], (8, LANES))
        curve = jnp.broadcast_to(curve_ref[pl.ds(row, 1), :], (8, LANES))
        mu = lam + curve
        ratio2 = jnp.exp(curve * (2.0 / (512.0 * 512.0)))
        columns = []
        for g in range(4):
            s = ((sub + 8.0 * g) * 16.0 + 0.5) * (1 / 512.0) - 0.5
            e = jnp.exp(mu * s + curve * (s * s))
            ratio = jnp.exp(mu * (1 / 512.0) + curve * ((2.0 * s + 1 / 512.0) * (1 / 512.0)))
            column = []
            for p in range(16):
                column.append(e)
                if p < 15:
                    e = e * ratio
                    ratio = ratio * ratio2
            columns.append(column)
        return jnp.concatenate([columns[g][p] for p in range(16) for g in range(4)], axis=0)

    def pair(row):
        e = jnp.concatenate([tile(row), tile(row + 1)], axis=1)
        e_high = e.astype(jnp.bfloat16)
        e_low = (e - e_high.astype(jnp.float32)).astype(jnp.bfloat16)
        sums = jnp.dot(left, e_high, preferred_element_type=jnp.float32)
        sums = sums + jnp.dot(left, e_low, preferred_element_type=jnp.float32)
        values = (sums[0:8] + sums[8:16]) / sums[16:24]
        return [values[:, :LANES], values[:, LANES:]]

    def body(t, _):
        values = pair(4 * t) + pair(4 * t + 2)
        rows = pl.ds(pl.multiple_of(8 * t, 8), 8)
        for x in range(4):
            block = jnp.concatenate([v[2 * x : 2 * x + 2] for v in values], axis=0)
            for y in range(4):
                sent_ref[x, y, rows, :] = block
        return 0

    rows = lam_ref.shape[0]
    for x in range(4):
        for y in range(4):
            sent_ref[x, y, 2 * rows :, :] = lam_ref[...]
    lax.fori_loop(0, rows // 4, body, 0, unroll=4)


def species(lam, curve, table):
    rows = lam.shape[0]
    return pl.pallas_call(
        species_kernel,
        out_shape=jax.ShapeDtypeStruct((4, 4, 3 * rows, LANES), jnp.float32),
        in_specs=[pl.BlockSpec(memory_space=pltpu.VMEM)] * 3,
        out_specs=pl.BlockSpec(memory_space=pltpu.VMEM),
        scratch_shapes=[pltpu.VMEM((LANES, 32), jnp.float32)],
        cost_estimate=pl.CostEstimate(flops=6 * 10**9, bytes_accessed=1 << 19, transcendentals=0),
        compiler_params=pltpu.CompilerParams(vmem_limit_bytes=16 << 20),
        name="species",
    )(lam, curve, table)


def blocks_kernel(table_ref, out_ref, turned_ref):
    points = table_ref.shape[0]
    turned_ref[:, :points] = jnp.transpose(table_ref[...])
    block = [turned_ref[pl.ds(q, 8, stride=8), :points] for q in range(8)]
    block = jnp.concatenate(block, axis=1)
    out_ref[...] = jnp.broadcast_to(block[:, None, :], out_ref.shape)


def blocks(table):
    return pl.pallas_call(
        blocks_kernel,
        out_shape=jax.ShapeDtypeStruct((8, 4, LANES), jnp.float32),
        in_specs=[pl.BlockSpec(memory_space=pltpu.VMEM)],
        out_specs=pl.BlockSpec(memory_space=pltpu.VMEM),
        scratch_shapes=[pltpu.VMEM((64, LANES), jnp.float32)],
        compiler_params=pltpu.CompilerParams(vmem_limit_bytes=4 << 20),
        name="blocks",
    )(table)


def lay_kernel(flip, core_ref, blocks_ref, *refs):
    species_ref, lam_ref, sems = refs[-3:]
    rows = lam_ref.shape[3]
    core = core_ref[0] ^ flip
    copies = []
    for y in range(4):
        copies.append((blocks_ref.at[:, y, pl.ds(0, 2 * rows), :], species_ref.at[y, core]))
        copies.append((blocks_ref.at[:, y, pl.ds(2 * rows, rows), :], lam_ref.at[y, core]))
    started = [pltpu.make_async_copy(a, b, sems.at[i]) for i, (a, b) in enumerate(copies)]
    for copy in started:
        copy.start()
    for copy in started:
        copy.wait()


def lay(core, blocks, flip, laid=()):
    anywhere = pl.BlockSpec(memory_space=pl.ANY)
    rows = blocks.shape[2] // 3
    return pl.pallas_call(
        functools.partial(lay_kernel, flip),
        out_shape=[
            jax.ShapeDtypeStruct((4, 2, 4, 2 * rows, LANES), jnp.float32),
            jax.ShapeDtypeStruct((4, 2, 4, rows, LANES), jnp.float32),
        ],
        in_specs=[pl.BlockSpec(memory_space=pltpu.SMEM), pl.BlockSpec(memory_space=pltpu.VMEM)]
        + [anywhere] * len(laid),
        out_specs=[anywhere] * 2,
        input_output_aliases={2: 0, 3: 1} if laid else {},
        scratch_shapes=[pltpu.SemaphoreType.DMA((8,))],
        cost_estimate=pl.CostEstimate(flops=2 * 10**9, bytes_accessed=3 << 20, transcendentals=0),
        compiler_params=pltpu.CompilerParams(vmem_limit_bytes=4 << 20),
        name="lay",
    )(core, blocks, *laid)


def exchange(array, axes):
    return lax.all_to_all(array, axes, split_axis=0, concat_axis=0, tiled=True)


def per_device(slope, curvature, target_mean, target_var, table):
    x = lax.axis_index("x")
    core = jnp.reshape(lax.axis_index("core"), (1,)).astype(jnp.int32)
    points = exchange(blocks(table.T).reshape(32, LANES), ("z", "x"))

    size = slope.shape[0] // 4
    mine = [
        lax.dynamic_slice_in_dim(a, x * size, size, 0).reshape(-1, LANES)
        for a in (slope, curvature, target_mean, target_var)
    ]
    lam = newton(*mine)
    sent = species(lam, mine[1], points)
    own = exchange(sent.reshape(16, *sent.shape[2:]), ("x", "y")).reshape(sent.shape)
    other = lax.ppermute(own, "core", [(0, 1), (1, 0)])
    values, final_slope = lay(core, other, 1, lay(core, own, 0))
    values = jnp.transpose(values.reshape(-1, 2, LANES), (1, 0, 2)).reshape(2, -1)
    return values, final_slope.reshape(-1)


def solution(mesh):
    mesh = jax.sharding.Mesh(np.reshape(mesh.devices, (8, 4, 4, 2)), ("z", "x", "y", "core"))
    bins = P(("y", "core"))
    placed = (bins, bins, bins, bins, P(None, ("z", "x")))
    return jax.shard_map(
        per_device, mesh=mesh, in_specs=placed, out_specs=(P(("z", "x"), None), P()), check_vma=False
    )
```

```python
import functools

import jax
import jax.numpy as jnp
import numpy as np
from jax import lax
from jax.experimental import pallas as pl
from jax.experimental.pallas import tpu as pltpu
from jax.sharding import PartitionSpec as P

ITERS = 3
LANES = 128
EARLY = 6
COARSE = 8
FINE = 16


def weights(lam_ref, curve_ref, t):
    sub = lax.broadcasted_iota(jnp.int32, (8, LANES), 0).astype(jnp.float32)

    def tile(row):
        lam = jnp.broadcast_to(lam_ref[pl.ds(row, 1), :], (8, LANES))
        curve = jnp.broadcast_to(curve_ref[pl.ds(row, 1), :], (8, LANES))
        mu = lam + curve
        ratio2 = jnp.exp(curve * (2.0 / (512.0 * 512.0)))
        columns = []
        for g in range(4):
            s = ((sub + 8.0 * g) * 16.0 + 0.5) * (1 / 512.0) - 0.5
            e = jnp.exp(mu * s + curve * (s * s))
            ratio = jnp.exp(mu * (1 / 512.0) + curve * ((2.0 * s + 1 / 512.0) * (1 / 512.0)))
            column = []
            for p in range(16):
                column.append(e)
                if p < 15:
                    e = e * ratio
                    ratio = ratio * ratio2
            columns.append(column)
        return jnp.concatenate([columns[g][p] for p in range(16) for g in range(4)], axis=0)

    e = jnp.concatenate([tile(2 * t), tile(2 * t + 1)], axis=1)
    high = e.astype(jnp.bfloat16)
    return high, (e - high.astype(jnp.float32)).astype(jnp.bfloat16)


def newton_kernel(
    slope_ref, curve_ref, mean_ref, var_ref, lam_ref, high_ref, low_ref, ch_ref, sh_ref, g_ref
):
    def body(v, _):
        rows = pl.ds(pl.multiple_of(v * 8, 8), 8)
        curve = curve_ref[rows, :]
        mean = mean_ref[rows, :]
        inverse = 1.0 / var_ref[rows, :]
        for j in range(FINE):
            angle = curve * ((2 * j + 1) / 16384.0)
            up, down = jnp.exp(angle), jnp.exp(-angle)
            up2, down2 = up * up, down * down
            for i in range(COARSE):
                ch_ref[i * FINE + j] = 0.5 * (up + down)
                sh_ref[i * FINE + j] = 0.5 * (up - down)
                if i < COARSE - 1:
                    up, down = up * up2, down * down2
            g_ref[j] = jnp.exp(curve * (((2 * j + 1) / 1024.0) ** 2))
        for i in range(COARSE):
            g_ref[FINE + i] = jnp.exp(curve * (((2 * i + 1) / 32.0) ** 2))

        def newton(_, lam):
            mu = lam + curve
            up, down = jnp.exp(mu * (1 / 1024.0)), jnp.exp(mu * (-1 / 1024.0))
            up2, down2 = up * up, down * down
            sums = [[None] * 4 for _ in range(COARSE)]
            for j in range(FINE):
                g = g_ref[j]
                even, odd = g * (up + down), g * (up - down)
                d = (2 * j + 1) / 1024.0
                d_even, d_odd = even * d, odd * d
                for i in range(COARSE):
                    ch, sh = ch_ref[i * FINE + j], sh_ref[i * FINE + j]
                    terms = (ch * even, sh * odd, ch * d_odd, sh * d_even)
                    sums[i] = [t if s is None else s + t for s, t in zip(sums[i], terms)]
                if j < FINE - 1:
                    up, down = up * up2, down * down2
            up, down = jnp.exp(mu * (1 / 32.0)), jnp.exp(mu * (-1 / 32.0))
            up2, down2 = up * up, down * down
            partition, moment = 0.0, 0.0
            for i in range(COARSE):
                g = g_ref[FINE + i]
                even, odd = g * (up + down), g * (up - down)
                a = (2 * i + 1) / 32.0
                e0, o0, o1, e1 = sums[i]
                partition = partition + (even * e0 + odd * o0)
                moment = moment + (a * (odd * e0 + even * o0) + (even * o1 + odd * e1))
                if i < COARSE - 1:
                    up, down = up * up2, down * down2
            return lam + (mean - (0.5 + moment / partition)) * inverse

        lam_ref[rows, :] = lax.fori_loop(0, ITERS, newton, slope_ref[rows, :])
        return 0

    lax.fori_loop(0, lam_ref.shape[0] // 8, body, 0)

    def early(t, _):
        high_ref[t], low_ref[t] = weights(lam_ref, curve_ref, t)
        return 0

    lax.fori_loop(0, EARLY, early, 0, unroll=EARLY // 2)


def newton(slope, curve, mean, var):
    part = jax.ShapeDtypeStruct((EARLY, 512, 2 * LANES), jnp.bfloat16)
    return pl.pallas_call(
        newton_kernel,
        out_shape=[jax.ShapeDtypeStruct(slope.shape, jnp.float32), part, part],
        in_specs=[pl.BlockSpec(memory_space=pltpu.VMEM)] * 4,
        out_specs=[pl.BlockSpec(memory_space=pltpu.VMEM)] * 3,
        scratch_shapes=[pltpu.VMEM((COARSE * FINE, 8, LANES), jnp.float32)] * 2
        + [pltpu.VMEM((COARSE + FINE, 8, LANES), jnp.float32)],
        cost_estimate=pl.CostEstimate(flops=12 * 10**9, bytes_accessed=1 << 18, transcendentals=0),
        compiler_params=pltpu.CompilerParams(vmem_limit_bytes=12 << 20),
        name="newton",
    )(slope, curve, mean, var)


def species_kernel(lam_ref, curve_ref, high_ref, low_ref, table_ref, sent_ref, turned_ref):
    turned_ref[...] = jnp.transpose(table_ref[...])
    table = jnp.concatenate([turned_ref[pl.ds(p, 8, stride=16), :] for p in range(16)], axis=1)
    high = table.astype(jnp.bfloat16).astype(jnp.float32)
    ones = jnp.ones((16, table.shape[1]), jnp.float32)
    left = jnp.concatenate([high, table - high, ones], axis=0).astype(jnp.bfloat16)
    def pair(high, low):
        sums = jnp.dot(left, high, preferred_element_type=jnp.float32)
        sums = sums + jnp.dot(left, low, preferred_element_type=jnp.float32)
        values = (sums[0:8] + sums[8:16]) / sums[16:24]
        return [values[:, :LANES], values[:, LANES:]]

    def store(t, values):
        rows = pl.ds(pl.multiple_of(8 * t, 8), 8)
        for x in range(4):
            block = jnp.concatenate([v[2 * x : 2 * x + 2] for v in values], axis=0)
            for y in range(4):
                sent_ref[x, y, rows, :] = block

    def early(t, _):
        store(t, [v for n in (2 * t, 2 * t + 1) for v in pair(high_ref[n], low_ref[n])])
        return 0

    def late(t, _):
        pairs = (weights(lam_ref, curve_ref, 2 * t + n) for n in range(2))
        store(t, [v for p in pairs for v in pair(*p)])
        return 0

    rows = lam_ref.shape[0]
    for x in range(4):
        for y in range(4):
            sent_ref[x, y, 2 * rows :, :] = lam_ref[...]
    first = EARLY // 2
    lax.fori_loop(0, first, early, 0, unroll=first)
    late(first, 0)
    lax.fori_loop(first + 1, rows // 4, late, 0, unroll=4)


def species(lam, curve, early, table):
    rows = lam.shape[0]
    return pl.pallas_call(
        species_kernel,
        out_shape=jax.ShapeDtypeStruct((4, 4, 3 * rows, LANES), jnp.float32),
        in_specs=[pl.BlockSpec(memory_space=pltpu.VMEM)] * 5,
        out_specs=pl.BlockSpec(memory_space=pltpu.VMEM),
        scratch_shapes=[pltpu.VMEM((LANES, 32), jnp.float32)],
        cost_estimate=pl.CostEstimate(flops=6 * 10**9, bytes_accessed=1 << 19, transcendentals=0),
        compiler_params=pltpu.CompilerParams(vmem_limit_bytes=16 << 20),
        name="species",
    )(lam, curve, *early, table)


def blocks_kernel(table_ref, out_ref, turned_ref):
    points = table_ref.shape[0]
    turned_ref[:, :points] = jnp.transpose(table_ref[...])
    block = [turned_ref[pl.ds(q, 8, stride=8), :points] for q in range(8)]
    block = jnp.concatenate(block, axis=1)
    out_ref[...] = jnp.broadcast_to(block[:, None, :], out_ref.shape)


def blocks(table):
    return pl.pallas_call(
        blocks_kernel,
        out_shape=jax.ShapeDtypeStruct((8, 4, LANES), jnp.float32),
        in_specs=[pl.BlockSpec(memory_space=pltpu.VMEM)],
        out_specs=pl.BlockSpec(memory_space=pltpu.VMEM),
        scratch_shapes=[pltpu.VMEM((64, LANES), jnp.float32)],
        name="blocks",
    )(table)


def lay_kernel(flip, core_ref, blocks_ref, *refs):
    species_ref, lam_ref, sems = refs[-3:]
    rows = lam_ref.shape[3]
    core = core_ref[0] ^ flip
    copies = []
    for y in range(4):
        copies.append((blocks_ref.at[:, y, pl.ds(0, 2 * rows), :], species_ref.at[y, core]))
        copies.append((blocks_ref.at[:, y, pl.ds(2 * rows, rows), :], lam_ref.at[y, core]))
    started = [pltpu.make_async_copy(a, b, sems.at[i]) for i, (a, b) in enumerate(copies)]
    for copy in started:
        copy.start()
    for copy in started:
        copy.wait()


def lay(core, blocks, flip, laid=()):
    anywhere = pl.BlockSpec(memory_space=pl.ANY)
    rows = blocks.shape[2] // 3
    return pl.pallas_call(
        functools.partial(lay_kernel, flip),
        out_shape=[
            jax.ShapeDtypeStruct((4, 2, 4, 2 * rows, LANES), jnp.float32),
            jax.ShapeDtypeStruct((4, 2, 4, rows, LANES), jnp.float32),
        ],
        in_specs=[pl.BlockSpec(memory_space=pltpu.SMEM), pl.BlockSpec(memory_space=pltpu.VMEM)]
        + [anywhere] * len(laid),
        out_specs=[anywhere] * 2,
        input_output_aliases={2: 0, 3: 1} if laid else {},
        scratch_shapes=[pltpu.SemaphoreType.DMA((8,))],
        cost_estimate=pl.CostEstimate(flops=2 * 10**9, bytes_accessed=3 << 20, transcendentals=0),
        compiler_params=pltpu.CompilerParams(vmem_limit_bytes=4 << 20),
        name="lay",
    )(core, blocks, *laid)


def exchange(array, axes):
    return lax.all_to_all(array, axes, split_axis=0, concat_axis=0, tiled=True)


def per_device(slope, curvature, target_mean, target_var, table):
    x = lax.axis_index("x")
    core = jnp.reshape(lax.axis_index("core"), (1,)).astype(jnp.int32)
    points = exchange(blocks(table.T).reshape(32, LANES), ("z", "x"))

    size = slope.shape[0] // 4
    mine = [
        lax.dynamic_slice_in_dim(a, x * size, size, 0).reshape(-1, LANES)
        for a in (slope, curvature, target_mean, target_var)
    ]
    lam, *early = newton(*mine)
    sent = species(lam, mine[1], early, points)
    own = exchange(sent.reshape(16, *sent.shape[2:]), ("x", "y")).reshape(sent.shape)
    other = lax.ppermute(own, "core", [(0, 1), (1, 0)])
    values, final_slope = lay(core, other, 1, lay(core, own, 0))
    values = jnp.transpose(values.reshape(-1, 2, LANES), (1, 0, 2)).reshape(2, -1)
    return values, final_slope.reshape(-1)


def solution(mesh):
    mesh = jax.sharding.Mesh(np.reshape(mesh.devices, (8, 4, 4, 2)), ("z", "x", "y", "core"))
    bins = P(("y", "core"))
    placed = (bins, bins, bins, bins, P(None, ("z", "x")))
    return jax.shard_map(
        per_device, mesh=mesh, in_specs=placed, out_specs=(P(("z", "x"), None), P()), check_vma=False
    )
```

```python
import functools

import jax
import jax.numpy as jnp
import numpy as np
from jax import lax
from jax.experimental import pallas as pl
from jax.experimental.pallas import tpu as pltpu
from jax.sharding import PartitionSpec as P

ITERS = 3
LANES = 128
COARSE = 8
FINE = 16


def newton_kernel(slope_ref, curve_ref, mean_ref, var_ref, lam_ref, ch_ref, sh_ref, g_ref):
    def body(v, _):
        rows = pl.ds(pl.multiple_of(v * 8, 8), 8)
        curve = curve_ref[rows, :]
        mean = mean_ref[rows, :]
        inverse = 1.0 / var_ref[rows, :]
        for j in range(FINE):
            angle = curve * ((2 * j + 1) / 16384.0)
            up, down = jnp.exp(angle), jnp.exp(-angle)
            up2, down2 = up * up, down * down
            for i in range(COARSE):
                ch_ref[i * FINE + j] = 0.5 * (up + down)
                sh_ref[i * FINE + j] = 0.5 * (up - down)
                if i < COARSE - 1:
                    up, down = up * up2, down * down2
            g_ref[j] = jnp.exp(curve * (((2 * j + 1) / 1024.0) ** 2))
        for i in range(COARSE):
            g_ref[FINE + i] = jnp.exp(curve * (((2 * i + 1) / 32.0) ** 2))

        def newton(_, lam):
            mu = lam + curve
            up, down = jnp.exp(mu * (1 / 1024.0)), jnp.exp(mu * (-1 / 1024.0))
            up2, down2 = up * up, down * down
            sums = [[None] * 4 for _ in range(COARSE)]
            for j in range(FINE):
                g = g_ref[j]
                even, odd = g * (up + down), g * (up - down)
                d = (2 * j + 1) / 1024.0
                d_even, d_odd = even * d, odd * d
                for i in range(COARSE):
                    ch, sh = ch_ref[i * FINE + j], sh_ref[i * FINE + j]
                    terms = (ch * even, sh * odd, ch * d_odd, sh * d_even)
                    sums[i] = [t if s is None else s + t for s, t in zip(sums[i], terms)]
                if j < FINE - 1:
                    up, down = up * up2, down * down2
            up, down = jnp.exp(mu * (1 / 32.0)), jnp.exp(mu * (-1 / 32.0))
            up2, down2 = up * up, down * down
            partition, moment = 0.0, 0.0
            for i in range(COARSE):
                g = g_ref[FINE + i]
                even, odd = g * (up + down), g * (up - down)
                a = (2 * i + 1) / 32.0
                e0, o0, o1, e1 = sums[i]
                partition = partition + (even * e0 + odd * o0)
                moment = moment + (a * (odd * e0 + even * o0) + (even * o1 + odd * e1))
                if i < COARSE - 1:
                    up, down = up * up2, down * down2
            return lam + (mean - (0.5 + moment / partition)) * inverse

        lam_ref[rows, :] = lax.fori_loop(0, ITERS, newton, slope_ref[rows, :])
        return 0

    lax.fori_loop(0, lam_ref.shape[0] // 8, body, 0)


def newton(slope, curve, mean, var):
    return pl.pallas_call(
        newton_kernel,
        out_shape=jax.ShapeDtypeStruct(slope.shape, jnp.float32),
        in_specs=[pl.BlockSpec(memory_space=pltpu.VMEM)] * 4,
        out_specs=pl.BlockSpec(memory_space=pltpu.VMEM),
        scratch_shapes=[pltpu.VMEM((COARSE * FINE, 8, LANES), jnp.float32)] * 2
        + [pltpu.VMEM((COARSE + FINE, 8, LANES), jnp.float32)],
        cost_estimate=pl.CostEstimate(flops=12 * 10**9, bytes_accessed=1 << 18, transcendentals=0),
        compiler_params=pltpu.CompilerParams(vmem_limit_bytes=8 << 20),
        name="newton",
    )(slope, curve, mean, var)


def species_kernel(lam_ref, curve_ref, table_ref, sent_ref, done_ref, turned_ref):
    turned_ref[...] = jnp.transpose(table_ref[...])
    table = jnp.concatenate([turned_ref[pl.ds(p, 8, stride=16), :] for p in range(16)], axis=1)
    high = table.astype(jnp.bfloat16).astype(jnp.float32)
    ones = jnp.ones((16, table.shape[1]), jnp.float32)
    left = jnp.concatenate([high, table - high, ones], axis=0).astype(jnp.bfloat16)
    sub = lax.broadcasted_iota(jnp.int32, (8, LANES), 0).astype(jnp.float32)

    def tile(row):
        lam = jnp.broadcast_to(lam_ref[pl.ds(row, 1), :], (8, LANES))
        curve = jnp.broadcast_to(curve_ref[pl.ds(row, 1), :], (8, LANES))
        mu = lam + curve
        ratio2 = jnp.exp(curve * (2.0 / (512.0 * 512.0)))
        columns = []
        for g in range(4):
            s = ((sub + 8.0 * g) * 16.0 + 0.5) * (1 / 512.0) - 0.5
            e = jnp.exp(mu * s + curve * (s * s))
            ratio = jnp.exp(mu * (1 / 512.0) + curve * ((2.0 * s + 1 / 512.0) * (1 / 512.0)))
            column = []
            for p in range(16):
                column.append(e)
                if p < 15:
                    e = e * ratio
                    ratio = ratio * ratio2
            columns.append(column)
        return jnp.concatenate([columns[g][p] for p in range(16) for g in range(4)], axis=0)

    def pair(row):
        e = jnp.concatenate([tile(row), tile(row + 1)], axis=1)
        e_high = e.astype(jnp.bfloat16)
        e_low = (e - e_high.astype(jnp.float32)).astype(jnp.bfloat16)
        sums = jnp.dot(left, e_high, preferred_element_type=jnp.float32)
        sums = sums + jnp.dot(left, e_low, preferred_element_type=jnp.float32)
        values = (sums[0:8] + sums[8:16]) / sums[16:24]
        return [values[:, :LANES], values[:, LANES:]]

    def body(t, _):
        values = pair(4 * t) + pair(4 * t + 2)
        rows = pl.ds(pl.multiple_of(8 * t, 8), 8)
        for x in range(4):
            block = jnp.concatenate([v[2 * x : 2 * x + 2] for v in values], axis=0)
            for y in range(4):
                sent_ref[x, y, rows, :] = block
        return 0

    rows = lam_ref.shape[0]
    done_ref[...] = lam_ref[...]
    lax.fori_loop(0, rows // 4, body, 0, unroll=4)


def species(lam, curve, table):
    rows = lam.shape[0]
    return pl.pallas_call(
        species_kernel,
        out_shape=[
            jax.ShapeDtypeStruct((4, 4, 2 * rows, LANES), jnp.float32),
            jax.ShapeDtypeStruct(lam.shape, jnp.float32),
        ],
        in_specs=[pl.BlockSpec(memory_space=pltpu.VMEM)] * 3,
        out_specs=[pl.BlockSpec(memory_space=pltpu.VMEM)] * 2,
        scratch_shapes=[pltpu.VMEM((LANES, 32), jnp.float32)],
        cost_estimate=pl.CostEstimate(flops=6 * 10**9, bytes_accessed=1 << 19, transcendentals=0),
        compiler_params=pltpu.CompilerParams(vmem_limit_bytes=16 << 20),
        name="species",
    )(lam, curve, table)


def blocks_kernel(table_ref, out_ref, turned_ref):
    points = table_ref.shape[0]
    turned_ref[:, :points] = jnp.transpose(table_ref[...])
    block = [turned_ref[pl.ds(q, 8, stride=8), :points] for q in range(8)]
    block = jnp.concatenate(block, axis=1)
    out_ref[...] = jnp.broadcast_to(block[:, None, :], out_ref.shape)


def blocks(table):
    return pl.pallas_call(
        blocks_kernel,
        out_shape=jax.ShapeDtypeStruct((8, 4, LANES), jnp.float32),
        in_specs=[pl.BlockSpec(memory_space=pltpu.VMEM)],
        out_specs=pl.BlockSpec(memory_space=pltpu.VMEM),
        scratch_shapes=[pltpu.VMEM((64, LANES), jnp.float32)],
        compiler_params=pltpu.CompilerParams(vmem_limit_bytes=4 << 20),
        name="blocks",
    )(table)


def lay_kernel(flip, by_xor, place_ref, blocks_ref, *refs):
    out_ref, sems = refs[-2:]
    x, y, core = place_ref[0], place_ref[1], place_ref[2] ^ flip
    started = []
    for e in range(4):
        if by_xor:
            pairs = [(blocks_ref.at[e, d], out_ref.at[y ^ e, core, x ^ d]) for d in range(4)]
        else:
            pairs = [(blocks_ref.at[:, e], out_ref.at[e, core])]
        started += [pltpu.make_async_copy(a, b, sems.at[e, d]) for d, (a, b) in enumerate(pairs)]
    for copy in started:
        copy.start()
    for copy in started:
        copy.wait()


def lay(place, blocks, flip, by_xor, laid=()):
    anywhere = pl.BlockSpec(memory_space=pl.ANY)
    return pl.pallas_call(
        functools.partial(lay_kernel, flip, by_xor),
        out_shape=jax.ShapeDtypeStruct((4, 2, 4, *blocks.shape[2:]), jnp.float32),
        in_specs=[pl.BlockSpec(memory_space=pltpu.SMEM), pl.BlockSpec(memory_space=pltpu.VMEM)]
        + [anywhere] * len(laid),
        out_specs=anywhere,
        input_output_aliases={2: 0} if laid else {},
        scratch_shapes=[pltpu.SemaphoreType.DMA((4, 4))],
        cost_estimate=pl.CostEstimate(
            flops=10**6 if by_xor else 2 * 10**9, bytes_accessed=1 << 10 if by_xor else 3 << 20, transcendentals=0
        ),
        compiler_params=pltpu.CompilerParams(vmem_limit_bytes=4 << 20),
        name="lay",
    )(place, blocks, *laid)


def with_partners(block, axis):
    others = [lax.ppermute(block, axis, [(i, i ^ d) for i in range(4)]) for d in (1, 2, 3)]
    return jnp.stack([block, *others])


def swap_and_lay(place, own, by_xor):
    other = lax.ppermute(own, "core", [(0, 1), (1, 0)])
    return lay(place, other, 1, by_xor, (lay(place, own, 0, by_xor),))


def exchange(array, axes):
    return lax.all_to_all(array, axes, split_axis=0, concat_axis=0, tiled=True)


def per_device(slope, curvature, target_mean, target_var, table):
    x = lax.axis_index("x")
    place = jnp.stack([x, lax.axis_index("y"), lax.axis_index("core")]).astype(jnp.int32)
    points = exchange(blocks(table.T).reshape(32, LANES), ("z", "x"))

    size = slope.shape[0] // 4
    mine = [
        lax.dynamic_slice_in_dim(a, x * size, size, 0).reshape(-1, LANES)
        for a in (slope, curvature, target_mean, target_var)
    ]
    lam = newton(*mine)
    sent, lam = species(lam, mine[1], points)
    own = exchange(sent.reshape(16, *sent.shape[2:]), ("x", "y")).reshape(sent.shape)
    final_slope = swap_and_lay(place, with_partners(with_partners(lam, "x"), "y"), True)
    own, final_slope = lax.optimization_barrier((own, final_slope))
    values = swap_and_lay(place, own, False)
    values = jnp.transpose(values.reshape(-1, 2, LANES), (1, 0, 2)).reshape(2, -1)
    return values, final_slope.reshape(-1)


def solution(mesh):
    mesh = jax.sharding.Mesh(np.reshape(mesh.devices, (8, 4, 4, 2)), ("z", "x", "y", "core"))
    bins = P(("y", "core"))
    placed = (bins, bins, bins, bins, P(None, ("z", "x")))
    return jax.shard_map(
        per_device, mesh=mesh, in_specs=placed, out_specs=(P(("z", "x"), None), P()), check_vma=False
    )
```

```python
import functools

import jax
import jax.numpy as jnp
import numpy as np
from jax import lax
from jax.experimental import pallas as pl
from jax.experimental.pallas import tpu as pltpu
from jax.sharding import PartitionSpec as P

ITERS = 3
LANES = 128
COARSE = 8
FINE = 16


def newton_kernel(slope_ref, curve_ref, mean_ref, var_ref, lam_ref, ch_ref, sh_ref, g_ref):
    def body(v, _):
        rows = pl.ds(pl.multiple_of(v * 8, 8), 8)
        curve = curve_ref[rows, :]
        mean = mean_ref[rows, :]
        inverse = 1.0 / var_ref[rows, :]
        for j in range(FINE):
            angle = curve * ((2 * j + 1) / 16384.0)
            up, down = jnp.exp(angle), jnp.exp(-angle)
            up2, down2 = up * up, down * down
            for i in range(COARSE):
                ch_ref[i * FINE + j] = 0.5 * (up + down)
                sh_ref[i * FINE + j] = 0.5 * (up - down)
                if i < COARSE - 1:
                    up, down = up * up2, down * down2
            g_ref[j] = jnp.exp(curve * (((2 * j + 1) / 1024.0) ** 2))
        for i in range(COARSE):
            g_ref[FINE + i] = jnp.exp(curve * (((2 * i + 1) / 32.0) ** 2))

        def newton(_, lam):
            mu = lam + curve
            up, down = jnp.exp(mu * (1 / 1024.0)), jnp.exp(mu * (-1 / 1024.0))
            up2, down2 = up * up, down * down
            sums = [[None] * 4 for _ in range(COARSE)]
            for j in range(FINE):
                g = g_ref[j]
                even, odd = g * (up + down), g * (up - down)
                d = (2 * j + 1) / 1024.0
                d_even, d_odd = even * d, odd * d
                for i in range(COARSE):
                    ch, sh = ch_ref[i * FINE + j], sh_ref[i * FINE + j]
                    terms = (ch * even, sh * odd, ch * d_odd, sh * d_even)
                    sums[i] = [t if s is None else s + t for s, t in zip(sums[i], terms)]
                if j < FINE - 1:
                    up, down = up * up2, down * down2
            up, down = jnp.exp(mu * (1 / 32.0)), jnp.exp(mu * (-1 / 32.0))
            up2, down2 = up * up, down * down
            partition, moment = 0.0, 0.0
            for i in range(COARSE):
                g = g_ref[FINE + i]
                even, odd = g * (up + down), g * (up - down)
                a = (2 * i + 1) / 32.0
                e0, o0, o1, e1 = sums[i]
                partition = partition + (even * e0 + odd * o0)
                moment = moment + (a * (odd * e0 + even * o0) + (even * o1 + odd * e1))
                if i < COARSE - 1:
                    up, down = up * up2, down * down2
            return lam + (mean - (0.5 + moment / partition)) * inverse

        lam_ref[rows, :] = lax.fori_loop(0, ITERS, newton, slope_ref[rows, :])
        return 0

    lax.fori_loop(0, lam_ref.shape[0] // 8, body, 0)


def newton(slope, curve, mean, var):
    return pl.pallas_call(
        newton_kernel,
        out_shape=jax.ShapeDtypeStruct(slope.shape, jnp.float32),
        in_specs=[pl.BlockSpec(memory_space=pltpu.VMEM)] * 4,
        out_specs=pl.BlockSpec(memory_space=pltpu.VMEM),
        scratch_shapes=[pltpu.VMEM((COARSE * FINE, 8, LANES), jnp.float32)] * 2
        + [pltpu.VMEM((COARSE + FINE, 8, LANES), jnp.float32)],
        cost_estimate=pl.CostEstimate(flops=12 * 10**9, bytes_accessed=1 << 18, transcendentals=0),
        compiler_params=pltpu.CompilerParams(vmem_limit_bytes=8 << 20),
        name="newton",
    )(slope, curve, mean, var)


def species_kernel(lam_ref, curve_ref, table_ref, sent_ref, turned_ref):
    turned_ref[...] = jnp.transpose(table_ref[...])
    table = jnp.concatenate([turned_ref[pl.ds(p, 8, stride=16), :] for p in range(16)], axis=1)
    high = table.astype(jnp.bfloat16).astype(jnp.float32)
    ones = jnp.ones((8, table.shape[1]), jnp.float32)
    for_high = jnp.concatenate([high, ones, table - high], axis=0).astype(jnp.bfloat16)
    for_low = jnp.concatenate([high, ones], axis=0).astype(jnp.bfloat16)
    sub = lax.broadcasted_iota(jnp.int32, (8, LANES), 0).astype(jnp.float32)

    def tile(row):
        lam = jnp.broadcast_to(lam_ref[pl.ds(row, 1), :], (8, LANES))
        curve = jnp.broadcast_to(curve_ref[pl.ds(row, 1), :], (8, LANES))
        mu = lam + curve
        ratio2 = jnp.exp(curve * (2.0 / (512.0 * 512.0)))
        columns = []
        for g in range(4):
            s = ((sub + 8.0 * g) * 16.0 + 0.5) * (1 / 512.0) - 0.5
            e = jnp.exp(mu * s + curve * (s * s))
            ratio = jnp.exp(mu * (1 / 512.0) + curve * ((2.0 * s + 1 / 512.0) * (1 / 512.0)))
            column = []
            for p in range(16):
                column.append(e)
                if p < 15:
                    e = e * ratio
                    ratio = ratio * ratio2
            columns.append(column)
        return jnp.concatenate([columns[g][p] for p in range(16) for g in range(4)], axis=0)

    def pair(row):
        e = jnp.concatenate([tile(row), tile(row + 1)], axis=1)
        e_high = e.astype(jnp.bfloat16)
        e_low = (e - e_high.astype(jnp.float32)).astype(jnp.bfloat16)
        sums = jnp.dot(for_high, e_high, preferred_element_type=jnp.float32)
        more = jnp.dot(for_low, e_low, preferred_element_type=jnp.float32)
        values = (sums[0:8] + sums[16:24] + more[0:8]) / (sums[8:16] + more[8:16])
        return [values[:, :LANES], values[:, LANES:]]

    def body(t, _):
        values = pair(4 * t) + pair(4 * t + 2)
        rows = pl.ds(pl.multiple_of(8 * t, 8), 8)
        for x in range(4):
            block = jnp.concatenate([v[2 * x : 2 * x + 2] for v in values], axis=0)
            for y in range(4):
                sent_ref[x, y, rows, :] = block
        return 0

    rows = lam_ref.shape[0]
    for x in range(4):
        for y in range(4):
            sent_ref[x, y, 2 * rows :, :] = lam_ref[...]
    lax.fori_loop(0, rows // 4, body, 0, unroll=16)


def species(lam, curve, table):
    rows = lam.shape[0]
    return pl.pallas_call(
        species_kernel,
        out_shape=jax.ShapeDtypeStruct((4, 4, 3 * rows, LANES), jnp.float32),
        in_specs=[pl.BlockSpec(memory_space=pltpu.VMEM)] * 3,
        out_specs=pl.BlockSpec(memory_space=pltpu.VMEM),
        scratch_shapes=[pltpu.VMEM((LANES, 32), jnp.float32)],
        cost_estimate=pl.CostEstimate(flops=6 * 10**9, bytes_accessed=1 << 19, transcendentals=0),
        compiler_params=pltpu.CompilerParams(vmem_limit_bytes=16 << 20),
        name="species",
    )(lam, curve, table)


def blocks_kernel(table_ref, out_ref, turned_ref):
    points = table_ref.shape[0]
    turned_ref[:, :points] = jnp.transpose(table_ref[...])
    block = [turned_ref[pl.ds(q, 8, stride=8), :points] for q in range(8)]
    block = jnp.concatenate(block, axis=1)
    out_ref[...] = jnp.broadcast_to(block[:, None, :], out_ref.shape)


def blocks(table):
    return pl.pallas_call(
        blocks_kernel,
        out_shape=jax.ShapeDtypeStruct((8, 4, LANES), jnp.float32),
        in_specs=[pl.BlockSpec(memory_space=pltpu.VMEM)],
        out_specs=pl.BlockSpec(memory_space=pltpu.VMEM),
        scratch_shapes=[pltpu.VMEM((64, LANES), jnp.float32)],
        compiler_params=pltpu.CompilerParams(vmem_limit_bytes=4 << 20),
        name="blocks",
    )(table)


def lay_kernel(flip, core_ref, blocks_ref, *refs):
    species_ref, lam_ref, sems = refs[-3:]
    rows = lam_ref.shape[3]
    core = core_ref[0] ^ flip
    copies = []
    for y in range(4):
        copies.append((blocks_ref.at[:, y, pl.ds(0, 2 * rows), :], species_ref.at[y, core]))
        copies.append((blocks_ref.at[:, y, pl.ds(2 * rows, rows), :], lam_ref.at[y, core]))
    started = [pltpu.make_async_copy(a, b, sems.at[i]) for i, (a, b) in enumerate(copies)]
    for copy in started:
        copy.start()
    for copy in started:
        copy.wait()


def lay(core, blocks, flip, laid=()):
    anywhere = pl.BlockSpec(memory_space=pl.ANY)
    rows = blocks.shape[2] // 3
    return pl.pallas_call(
        functools.partial(lay_kernel, flip),
        out_shape=[
            jax.ShapeDtypeStruct((4, 2, 4, 2 * rows, LANES), jnp.float32),
            jax.ShapeDtypeStruct((4, 2, 4, rows, LANES), jnp.float32),
        ],
        in_specs=[pl.BlockSpec(memory_space=pltpu.SMEM), pl.BlockSpec(memory_space=pltpu.VMEM)]
        + [anywhere] * len(laid),
        out_specs=[anywhere] * 2,
        input_output_aliases={2: 0, 3: 1} if laid else {},
        scratch_shapes=[pltpu.SemaphoreType.DMA((8,))],
        cost_estimate=pl.CostEstimate(flops=2 * 10**9, bytes_accessed=3 << 20, transcendentals=0),
        compiler_params=pltpu.CompilerParams(vmem_limit_bytes=4 << 20),
        name="lay",
    )(core, blocks, *laid)


def exchange(array, axes):
    return lax.all_to_all(array, axes, split_axis=0, concat_axis=0, tiled=True)


def per_device(slope, curvature, target_mean, target_var, table):
    x = lax.axis_index("x")
    core = jnp.reshape(lax.axis_index("core"), (1,)).astype(jnp.int32)
    points = exchange(blocks(table.T).reshape(32, LANES), ("z", "x"))

    size = slope.shape[0] // 4
    mine = [
        lax.dynamic_slice_in_dim(a, x * size, size, 0).reshape(-1, LANES)
        for a in (slope, curvature, target_mean, target_var)
    ]
    lam = newton(*mine)
    sent = species(lam, mine[1], points)
    own = exchange(sent.reshape(16, *sent.shape[2:]), ("x", "y")).reshape(sent.shape)
    other = lax.ppermute(own, "core", [(0, 1), (1, 0)])
    values, final_slope = lay(core, other, 1, lay(core, own, 0))
    values = jnp.transpose(values.reshape(-1, 2, LANES), (1, 0, 2)).reshape(2, -1)
    return values, final_slope.reshape(-1)


def solution(mesh):
    mesh = jax.sharding.Mesh(np.reshape(mesh.devices, (8, 4, 4, 2)), ("z", "x", "y", "core"))
    bins = P(("y", "core"))
    placed = (bins, bins, bins, bins, P(None, ("z", "x")))
    return jax.shard_map(
        per_device, mesh=mesh, in_specs=placed, out_specs=(P(("z", "x"), None), P()), check_vma=False
    )
```

```python
import functools

import jax
import jax.numpy as jnp
import numpy as np
from jax import lax
from jax.experimental import pallas as pl
from jax.experimental.pallas import tpu as pltpu
from jax.sharding import PartitionSpec as P

ITERS = 3
LANES = 128
COARSE = 8
FINE = 16


def newton_kernel(slope_ref, curve_ref, mean_ref, var_ref, lam_ref, ch_ref, sh_ref, g_ref):
    def body(v, _):
        rows = pl.ds(pl.multiple_of(v * 8, 8), 8)
        curve = curve_ref[rows, :]
        mean = mean_ref[rows, :]
        inverse = 1.0 / var_ref[rows, :]
        for j in range(FINE):
            angle = curve * ((2 * j + 1) / 16384.0)
            up, down = jnp.exp(angle), jnp.exp(-angle)
            up2, down2 = up * up, down * down
            for i in range(COARSE):
                ch_ref[i * FINE + j] = 0.5 * (up + down)
                sh_ref[i * FINE + j] = 0.5 * (up - down)
                if i < COARSE - 1:
                    up, down = up * up2, down * down2
            g_ref[j] = jnp.exp(curve * (((2 * j + 1) / 1024.0) ** 2))
        for i in range(COARSE):
            g_ref[FINE + i] = jnp.exp(curve * (((2 * i + 1) / 32.0) ** 2))

        def newton(_, lam):
            mu = lam + curve
            up, down = jnp.exp(mu * (1 / 1024.0)), jnp.exp(mu * (-1 / 1024.0))
            up2, down2 = up * up, down * down
            sums = [[None] * 4 for _ in range(COARSE)]
            for j in range(FINE):
                g = g_ref[j]
                even, odd = g * (up + down), g * (up - down)
                d = (2 * j + 1) / 1024.0
                d_even, d_odd = even * d, odd * d
                for i in range(COARSE):
                    ch, sh = ch_ref[i * FINE + j], sh_ref[i * FINE + j]
                    terms = (ch * even, sh * odd, ch * d_odd, sh * d_even)
                    sums[i] = [t if s is None else s + t for s, t in zip(sums[i], terms)]
                if j < FINE - 1:
                    up, down = up * up2, down * down2
            up, down = jnp.exp(mu * (1 / 32.0)), jnp.exp(mu * (-1 / 32.0))
            up2, down2 = up * up, down * down
            partition, moment = 0.0, 0.0
            for i in range(COARSE):
                g = g_ref[FINE + i]
                even, odd = g * (up + down), g * (up - down)
                a = (2 * i + 1) / 32.0
                e0, o0, o1, e1 = sums[i]
                partition = partition + (even * e0 + odd * o0)
                moment = moment + (a * (odd * e0 + even * o0) + (even * o1 + odd * e1))
                if i < COARSE - 1:
                    up, down = up * up2, down * down2
            return lam + (mean - (0.5 + moment / partition)) * inverse

        lam_ref[rows, :] = lax.fori_loop(0, ITERS, newton, slope_ref[rows, :])
        return 0

    lax.fori_loop(0, lam_ref.shape[0] // 8, body, 0)


def newton(slope, curve, mean, var):
    return pl.pallas_call(
        newton_kernel,
        out_shape=jax.ShapeDtypeStruct(slope.shape, jnp.float32),
        in_specs=[pl.BlockSpec(memory_space=pltpu.VMEM)] * 4,
        out_specs=pl.BlockSpec(memory_space=pltpu.VMEM),
        scratch_shapes=[pltpu.VMEM((COARSE * FINE, 8, LANES), jnp.float32)] * 2
        + [pltpu.VMEM((COARSE + FINE, 8, LANES), jnp.float32)],
        cost_estimate=pl.CostEstimate(flops=12 * 10**9, bytes_accessed=1 << 18, transcendentals=0),
        compiler_params=pltpu.CompilerParams(vmem_limit_bytes=8 << 20),
        name="newton",
    )(slope, curve, mean, var)


def species_kernel(lam_ref, curve_ref, table_ref, sent_ref, turned_ref):
    turned_ref[...] = jnp.transpose(table_ref[...])
    table = jnp.concatenate([turned_ref[pl.ds(p, 8, stride=16), :] for p in range(16)], axis=1)
    high = table.astype(jnp.bfloat16).astype(jnp.float32)
    ones = jnp.ones((8, table.shape[1]), jnp.float32)
    for_high = jnp.concatenate([high, ones, table - high], axis=0).astype(jnp.bfloat16)
    for_low = jnp.concatenate([high, ones], axis=0).astype(jnp.bfloat16)
    sub = lax.broadcasted_iota(jnp.int32, (8, LANES), 0).astype(jnp.float32)

    def tile(row):
        lam = jnp.broadcast_to(lam_ref[pl.ds(row, 1), :], (8, LANES))
        curve = jnp.broadcast_to(curve_ref[pl.ds(row, 1), :], (8, LANES))
        mu = lam + curve
        ratio2 = jnp.exp(curve * (2.0 / (512.0 * 512.0)))
        columns = []
        for g in range(4):
            s = ((sub + 8.0 * g) * 16.0 + 0.5) * (1 / 512.0) - 0.5
            e = jnp.exp(mu * s + curve * (s * s))
            ratio = jnp.exp(mu * (1 / 512.0) + curve * ((2.0 * s + 1 / 512.0) * (1 / 512.0)))
            column = []
            for p in range(16):
                column.append(e)
                if p < 15:
                    e = e * ratio
                    ratio = ratio * ratio2
            columns.append(column)
        return jnp.concatenate([columns[g][p] for p in range(16) for g in range(4)], axis=0)

    def pair(row):
        e = jnp.concatenate([tile(row), tile(row + 1)], axis=1)
        e_high = e.astype(jnp.bfloat16)
        e_low = (e - e_high.astype(jnp.float32)).astype(jnp.bfloat16)
        sums = jnp.dot(for_high, e_high, preferred_element_type=jnp.float32)
        more = jnp.dot(for_low, e_low, preferred_element_type=jnp.float32)
        values = (sums[0:8] + sums[16:24] + more[0:8]) / (sums[8:16] + more[8:16])
        return [values[:, :LANES], values[:, LANES:]]

    def body(t, _):
        values = pair(4 * t) + pair(4 * t + 2)
        rows = pl.ds(pl.multiple_of(8 * t, 8), 8)
        for x in range(4):
            block = jnp.concatenate([v[2 * x : 2 * x + 2] for v in values], axis=0)
            for y in range(4):
                sent_ref[y, x, rows, :] = block
        return 0

    rows = lam_ref.shape[0]
    for x in range(4):
        for y in range(4):
            sent_ref[y, x, 2 * rows :, :] = lam_ref[...]
    lax.fori_loop(0, rows // 4, body, 0, unroll=16)


def species(lam, curve, table):
    rows = lam.shape[0]
    return pl.pallas_call(
        species_kernel,
        out_shape=jax.ShapeDtypeStruct((4, 4, 3 * rows, LANES), jnp.float32),
        in_specs=[pl.BlockSpec(memory_space=pltpu.VMEM)] * 3,
        out_specs=pl.BlockSpec(memory_space=pltpu.VMEM),
        scratch_shapes=[pltpu.VMEM((LANES, 32), jnp.float32)],
        cost_estimate=pl.CostEstimate(flops=6 * 10**9, bytes_accessed=1 << 19, transcendentals=0),
        compiler_params=pltpu.CompilerParams(vmem_limit_bytes=16 << 20),
        name="species",
    )(lam, curve, table)


def blocks_kernel(table_ref, out_ref, turned_ref):
    points = table_ref.shape[0]
    turned_ref[:, :points] = jnp.transpose(table_ref[...])
    block = [turned_ref[pl.ds(q, 8, stride=8), :points] for q in range(8)]
    block = jnp.concatenate(block, axis=1)
    out_ref[...] = jnp.broadcast_to(block[:, None, :], out_ref.shape)


def blocks(table):
    return pl.pallas_call(
        blocks_kernel,
        out_shape=jax.ShapeDtypeStruct((8, 4, LANES), jnp.float32),
        in_specs=[pl.BlockSpec(memory_space=pltpu.VMEM)],
        out_specs=pl.BlockSpec(memory_space=pltpu.VMEM),
        scratch_shapes=[pltpu.VMEM((64, LANES), jnp.float32)],
        compiler_params=pltpu.CompilerParams(vmem_limit_bytes=4 << 20),
        name="blocks",
    )(table)


def lay_kernel(flip, core_ref, blocks_ref, *refs):
    species_ref, lam_ref, sems = refs[-3:]
    rows = lam_ref.shape[3]
    core = core_ref[0] ^ flip
    copies = [
        (blocks_ref.at[:, :, pl.ds(0, 2 * rows), :], species_ref.at[:, core]),
        (blocks_ref.at[:, :, pl.ds(2 * rows, rows), :], lam_ref.at[:, core]),
    ]
    started = [pltpu.make_async_copy(a, b, sems.at[i]) for i, (a, b) in enumerate(copies)]
    for copy in started:
        copy.start()
    for copy in started:
        copy.wait()


def lay(core, blocks, flip, laid=()):
    anywhere = pl.BlockSpec(memory_space=pl.ANY)
    rows = blocks.shape[2] // 3
    return pl.pallas_call(
        functools.partial(lay_kernel, flip),
        out_shape=[
            jax.ShapeDtypeStruct((4, 2, 4, 2 * rows, LANES), jnp.float32),
            jax.ShapeDtypeStruct((4, 2, 4, rows, LANES), jnp.float32),
        ],
        in_specs=[pl.BlockSpec(memory_space=pltpu.SMEM), pl.BlockSpec(memory_space=pltpu.VMEM)]
        + [anywhere] * len(laid),
        out_specs=[anywhere] * 2,
        input_output_aliases={2: 0, 3: 1} if laid else {},
        scratch_shapes=[pltpu.SemaphoreType.DMA((2,))],
        cost_estimate=pl.CostEstimate(flops=2 * 10**9, bytes_accessed=3 << 20, transcendentals=0),
        compiler_params=pltpu.CompilerParams(vmem_limit_bytes=4 << 20),
        name="lay",
    )(core, blocks, *laid)


def exchange(array, axes):
    return lax.all_to_all(array, axes, split_axis=0, concat_axis=0, tiled=True)


def per_device(slope, curvature, target_mean, target_var, table):
    x = lax.axis_index("x")
    core = jnp.reshape(lax.axis_index("core"), (1,)).astype(jnp.int32)
    points = exchange(blocks(table.T).reshape(32, LANES), ("z", "x"))

    size = slope.shape[0] // 4
    mine = [
        lax.dynamic_slice_in_dim(a, x * size, size, 0).reshape(-1, LANES)
        for a in (slope, curvature, target_mean, target_var)
    ]
    lam = newton(*mine)
    sent = species(lam, mine[1], points)
    own = exchange(sent.reshape(16, *sent.shape[2:]), ("y", "x")).reshape(sent.shape)
    other = lax.ppermute(own, "core", [(0, 1), (1, 0)])
    values, final_slope = lay(core, other, 1, lay(core, own, 0))
    values = jnp.transpose(values.reshape(-1, 2, LANES), (1, 0, 2)).reshape(2, -1)
    return values, final_slope.reshape(-1)


def solution(mesh):
    mesh = jax.sharding.Mesh(np.reshape(mesh.devices, (8, 4, 4, 2)), ("z", "x", "y", "core"))
    bins = P(("y", "core"))
    placed = (bins, bins, bins, bins, P(None, ("z", "x")))
    return jax.shard_map(
        per_device, mesh=mesh, in_specs=placed, out_specs=(P(("z", "x"), None), P()), check_vma=False
    )
```

```python
import functools

import jax
import jax.numpy as jnp
import numpy as np
from jax import lax
from jax.experimental import pallas as pl
from jax.experimental.pallas import tpu as pltpu
from jax.sharding import PartitionSpec as P

ITERS = 3
LANES = 128
COARSE = 8
FINE = 16


def newton_kernel(slope_ref, curve_ref, mean_ref, var_ref, lam_ref, ch_ref, sh_ref, g_ref):
    def body(v, _):
        rows = pl.ds(pl.multiple_of(v * 8, 8), 8)
        curve = curve_ref[rows, :]
        mean = mean_ref[rows, :]
        inverse = 1.0 / var_ref[rows, :]
        for j in range(FINE):
            angle = curve * ((2 * j + 1) / 16384.0)
            up, down = jnp.exp(angle), jnp.exp(-angle)
            up2, down2 = up * up, down * down
            for i in range(COARSE):
                ch_ref[i * FINE + j] = 0.5 * (up + down)
                sh_ref[i * FINE + j] = 0.5 * (up - down)
                if i < COARSE - 1:
                    up, down = up * up2, down * down2
            g_ref[j] = jnp.exp(curve * (((2 * j + 1) / 1024.0) ** 2))
        for i in range(COARSE):
            g_ref[FINE + i] = jnp.exp(curve * (((2 * i + 1) / 32.0) ** 2))

        def newton(_, lam):
            mu = lam + curve
            up, down = jnp.exp(mu * (1 / 1024.0)), jnp.exp(mu * (-1 / 1024.0))
            up2, down2 = up * up, down * down
            sums = [[None] * 4 for _ in range(COARSE)]
            for j in range(FINE):
                g = g_ref[j]
                even, odd = g * (up + down), g * (up - down)
                d = (2 * j + 1) / 1024.0
                d_even, d_odd = even * d, odd * d
                for i in range(COARSE):
                    ch, sh = ch_ref[i * FINE + j], sh_ref[i * FINE + j]
                    terms = (ch * even, sh * odd, ch * d_odd, sh * d_even)
                    sums[i] = [t if s is None else s + t for s, t in zip(sums[i], terms)]
                if j < FINE - 1:
                    up, down = up * up2, down * down2
            up, down = jnp.exp(mu * (1 / 32.0)), jnp.exp(mu * (-1 / 32.0))
            up2, down2 = up * up, down * down
            partition, moment = 0.0, 0.0
            for i in range(COARSE):
                g = g_ref[FINE + i]
                even, odd = g * (up + down), g * (up - down)
                a = (2 * i + 1) / 32.0
                e0, o0, o1, e1 = sums[i]
                partition = partition + (even * e0 + odd * o0)
                moment = moment + (a * (odd * e0 + even * o0) + (even * o1 + odd * e1))
                if i < COARSE - 1:
                    up, down = up * up2, down * down2
            return lam + (mean - (0.5 + moment / partition)) * inverse

        lam_ref[rows, :] = lax.fori_loop(0, ITERS, newton, slope_ref[rows, :])
        return 0

    lax.fori_loop(0, lam_ref.shape[0] // 8, body, 0)


def newton(slope, curve, mean, var):
    return pl.pallas_call(
        newton_kernel,
        out_shape=jax.ShapeDtypeStruct(slope.shape, jnp.float32),
        in_specs=[pl.BlockSpec(memory_space=pltpu.VMEM)] * 4,
        out_specs=pl.BlockSpec(memory_space=pltpu.VMEM),
        scratch_shapes=[pltpu.VMEM((COARSE * FINE, 8, LANES), jnp.float32)] * 2
        + [pltpu.VMEM((COARSE + FINE, 8, LANES), jnp.float32)],
        cost_estimate=pl.CostEstimate(flops=12 * 10**9, bytes_accessed=1 << 18, transcendentals=0),
        compiler_params=pltpu.CompilerParams(vmem_limit_bytes=8 << 20),
        name="newton",
    )(slope, curve, mean, var)


def species_kernel(lam_ref, curve_ref, table_ref, sent_ref, turned_ref):
    turned_ref[...] = jnp.transpose(table_ref[...])
    table = jnp.concatenate([turned_ref[pl.ds(p, 8, stride=16), :] for p in range(16)], axis=1)
    high = table.astype(jnp.bfloat16).astype(jnp.float32)
    ones = jnp.ones((8, table.shape[1]), jnp.float32)
    for_high = jnp.concatenate([high, ones, table - high], axis=0).astype(jnp.bfloat16)
    for_low = jnp.concatenate([high, ones], axis=0).astype(jnp.bfloat16)
    sub = lax.broadcasted_iota(jnp.int32, (8, LANES), 0).astype(jnp.float32)

    def tile(row):
        lam = jnp.broadcast_to(lam_ref[pl.ds(row, 1), :], (8, LANES))
        curve = jnp.broadcast_to(curve_ref[pl.ds(row, 1), :], (8, LANES))
        mu = lam + curve
        ratio2 = jnp.exp(curve * (2.0 / (512.0 * 512.0)))
        columns = []
        for g in range(4):
            s = ((sub + 8.0 * g) * 16.0 + 0.5) * (1 / 512.0) - 0.5
            e = jnp.exp(mu * s + curve * (s * s))
            ratio = jnp.exp(mu * (1 / 512.0) + curve * ((2.0 * s + 1 / 512.0) * (1 / 512.0)))
            column = []
            for p in range(16):
                column.append(e)
                if p < 15:
                    e = e * ratio
                    ratio = ratio * ratio2
            columns.append(column)
        return jnp.concatenate([columns[g][p] for p in range(16) for g in range(4)], axis=0)

    def pair(row):
        e = jnp.concatenate([tile(row), tile(row + 1)], axis=1)
        e_high = e.astype(jnp.bfloat16)
        e_low = (e - e_high.astype(jnp.float32)).astype(jnp.bfloat16)
        sums = jnp.dot(for_high, e_high, preferred_element_type=jnp.float32)
        more = jnp.dot(for_low, e_low, preferred_element_type=jnp.float32)
        values = (sums[0:8] + sums[16:24] + more[0:8]) / (sums[8:16] + more[8:16])
        return [values[:, :LANES], values[:, LANES:]]

    def body(t, _):
        values = pair(4 * t) + pair(4 * t + 2)
        rows = pl.ds(pl.multiple_of(8 * t, 8), 8)
        for x in range(4):
            block = jnp.concatenate([v[2 * x : 2 * x + 2] for v in values], axis=0)
            for y in range(4):
                sent_ref[y, x, rows, :] = block
        return 0

    rows = lam_ref.shape[0]
    for x in range(4):
        for y in range(4):
            sent_ref[y, x, 2 * rows :, :] = lam_ref[...]
    lax.fori_loop(0, rows // 4, body, 0, unroll=16)


def species(lam, curve, table):
    rows = lam.shape[0]
    return pl.pallas_call(
        species_kernel,
        out_shape=jax.ShapeDtypeStruct((4, 4, 3 * rows, LANES), jnp.float32),
        in_specs=[pl.BlockSpec(memory_space=pltpu.VMEM)] * 3,
        out_specs=pl.BlockSpec(memory_space=pltpu.VMEM),
        scratch_shapes=[pltpu.VMEM((LANES, 32), jnp.float32)],
        cost_estimate=pl.CostEstimate(flops=6 * 10**9, bytes_accessed=1 << 19, transcendentals=0),
        compiler_params=pltpu.CompilerParams(vmem_limit_bytes=16 << 20),
        name="species",
    )(lam, curve, table)


def blocks_kernel(table_ref, out_ref, near_ref, turned_ref, block_ref, sems):
    fetch = pltpu.make_async_copy(table_ref, near_ref, sems.at[0])
    fetch.start()
    fetch.wait()
    points = table_ref.shape[0]
    turned_ref[:, :points] = jnp.transpose(near_ref[...])
    block = [turned_ref[pl.ds(q, 8, stride=8), :points] for q in range(8)]
    block = jnp.concatenate(block, axis=1)
    block_ref[...] = jnp.broadcast_to(block[:, None, :], block_ref.shape)
    store = pltpu.make_async_copy(block_ref, out_ref, sems.at[1])
    store.start()
    store.wait()


def blocks(table):
    return pl.pallas_call(
        blocks_kernel,
        out_shape=jax.ShapeDtypeStruct((8, 4, LANES), jnp.float32),
        in_specs=[pl.BlockSpec(memory_space=pl.ANY)],
        out_specs=pl.BlockSpec(memory_space=pl.ANY),
        scratch_shapes=[
            pltpu.VMEM(table.shape, jnp.float32),
            pltpu.VMEM((64, LANES), jnp.float32),
            pltpu.VMEM((8, 4, LANES), jnp.float32),
            pltpu.SemaphoreType.DMA((2,)),
        ],
        name="blocks",
    )(table)


def lay_kernel(flip, core_ref, blocks_ref, *refs):
    species_ref, lam_ref, sems = refs[-3:]
    rows = lam_ref.shape[3]
    core = core_ref[0] ^ flip
    copies = [
        (blocks_ref.at[:, :, pl.ds(0, 2 * rows), :], species_ref.at[:, core]),
        (blocks_ref.at[:, :, pl.ds(2 * rows, rows), :], lam_ref.at[:, core]),
    ]
    started = [pltpu.make_async_copy(a, b, sems.at[i]) for i, (a, b) in enumerate(copies)]
    for copy in started:
        copy.start()
    for copy in started:
        copy.wait()


def lay(core, blocks, flip, laid=()):
    anywhere = pl.BlockSpec(memory_space=pl.ANY)
    rows = blocks.shape[2] // 3
    return pl.pallas_call(
        functools.partial(lay_kernel, flip),
        out_shape=[
            jax.ShapeDtypeStruct((4, 2, 4, 2 * rows, LANES), jnp.float32),
            jax.ShapeDtypeStruct((4, 2, 4, rows, LANES), jnp.float32),
        ],
        in_specs=[pl.BlockSpec(memory_space=pltpu.SMEM), pl.BlockSpec(memory_space=pltpu.VMEM)]
        + [anywhere] * len(laid),
        out_specs=[anywhere] * 2,
        input_output_aliases={2: 0, 3: 1} if laid else {},
        scratch_shapes=[pltpu.SemaphoreType.DMA((2,))],
        cost_estimate=pl.CostEstimate(flops=2 * 10**9, bytes_accessed=3 << 20, transcendentals=0),
        compiler_params=pltpu.CompilerParams(vmem_limit_bytes=4 << 20),
        name="lay",
    )(core, blocks, *laid)


def exchange(array, axes):
    return lax.all_to_all(array, axes, split_axis=0, concat_axis=0, tiled=True)


def per_device(slope, curvature, target_mean, target_var, table):
    x = lax.axis_index("x")
    core = jnp.reshape(lax.axis_index("core"), (1,)).astype(jnp.int32)
    points = exchange(blocks(table.T).reshape(32, LANES), ("z", "x"))

    size = slope.shape[0] // 4
    mine = [
        lax.dynamic_slice_in_dim(a, x * size, size, 0).reshape(-1, LANES)
        for a in (slope, curvature, target_mean, target_var)
    ]
    lam = newton(*mine)
    sent = species(lam, mine[1], points)
    own = exchange(sent.reshape(16, *sent.shape[2:]), ("y", "x")).reshape(sent.shape)
    other = lax.ppermute(own, "core", [(0, 1), (1, 0)])
    values, final_slope = lay(core, other, 1, lay(core, own, 0))
    values = jnp.transpose(values.reshape(-1, 2, LANES), (1, 0, 2)).reshape(2, -1)
    return values, final_slope.reshape(-1)


def solution(mesh):
    mesh = jax.sharding.Mesh(np.reshape(mesh.devices, (8, 4, 4, 2)), ("z", "x", "y", "core"))
    bins = P(("y", "core"))
    placed = (bins, bins, bins, bins, P(None, ("z", "x")))
    return jax.shard_map(
        per_device, mesh=mesh, in_specs=placed, out_specs=(P(("z", "x"), None), P()), check_vma=False
    )
```

```python
import functools

import jax
import jax.numpy as jnp
import numpy as np
from jax import lax
from jax.experimental import pallas as pl
from jax.experimental.pallas import tpu as pltpu
from jax.sharding import PartitionSpec as P

ITERS = 3
LANES = 128
COARSE = 8
FINE = 16


def newton_kernel(slope_ref, curve_ref, mean_ref, var_ref, lam_ref, ch_ref, sh_ref, g_ref):
    def body(v, _):
        rows = pl.ds(pl.multiple_of(v * 8, 8), 8)
        curve = curve_ref[rows, :]
        mean = mean_ref[rows, :]
        inverse = 1.0 / var_ref[rows, :]
        for j in range(FINE):
            angle = curve * ((2 * j + 1) / 16384.0)
            up, down = jnp.exp(angle), jnp.exp(-angle)
            up2, down2 = up * up, down * down
            for i in range(COARSE):
                ch_ref[i * FINE + j] = 0.5 * (up + down)
                sh_ref[i * FINE + j] = 0.5 * (up - down)
                if i < COARSE - 1:
                    up, down = up * up2, down * down2
            g_ref[j] = jnp.exp(curve * (((2 * j + 1) / 1024.0) ** 2))
        for i in range(COARSE):
            g_ref[FINE + i] = jnp.exp(curve * (((2 * i + 1) / 32.0) ** 2))

        def newton(_, lam):
            mu = lam + curve
            up, down = jnp.exp(mu * (1 / 1024.0)), jnp.exp(mu * (-1 / 1024.0))
            up2, down2 = up * up, down * down
            sums = [[None] * 4 for _ in range(COARSE)]
            for j in range(FINE):
                g = g_ref[j]
                even, odd = g * (up + down), g * (up - down)
                d = (2 * j + 1) / 1024.0
                d_even, d_odd = even * d, odd * d
                for i in range(COARSE):
                    ch, sh = ch_ref[i * FINE + j], sh_ref[i * FINE + j]
                    terms = (ch * even, sh * odd, ch * d_odd, sh * d_even)
                    sums[i] = [t if s is None else s + t for s, t in zip(sums[i], terms)]
                if j < FINE - 1:
                    up, down = up * up2, down * down2
            up, down = jnp.exp(mu * (1 / 32.0)), jnp.exp(mu * (-1 / 32.0))
            up2, down2 = up * up, down * down
            partition, moment = 0.0, 0.0
            for i in range(COARSE):
                g = g_ref[FINE + i]
                even, odd = g * (up + down), g * (up - down)
                a = (2 * i + 1) / 32.0
                e0, o0, o1, e1 = sums[i]
                partition = partition + (even * e0 + odd * o0)
                moment = moment + (a * (odd * e0 + even * o0) + (even * o1 + odd * e1))
                if i < COARSE - 1:
                    up, down = up * up2, down * down2
            return lam + (mean - (0.5 + moment / partition)) * inverse

        lam_ref[rows, :] = lax.fori_loop(0, ITERS, newton, slope_ref[rows, :])
        return 0

    lax.fori_loop(0, lam_ref.shape[0] // 8, body, 0)


def newton(slope, curve, mean, var):
    return pl.pallas_call(
        newton_kernel,
        out_shape=jax.ShapeDtypeStruct(slope.shape, jnp.float32),
        in_specs=[pl.BlockSpec(memory_space=pltpu.VMEM)] * 4,
        out_specs=pl.BlockSpec(memory_space=pltpu.VMEM),
        scratch_shapes=[pltpu.VMEM((COARSE * FINE, 8, LANES), jnp.float32)] * 2
        + [pltpu.VMEM((COARSE + FINE, 8, LANES), jnp.float32)],
        cost_estimate=pl.CostEstimate(flops=12 * 10**9, bytes_accessed=1 << 18, transcendentals=0),
        compiler_params=pltpu.CompilerParams(vmem_limit_bytes=8 << 20),
        name="newton",
    )(slope, curve, mean, var)


def species_kernel(lam_ref, curve_ref, table_ref, sent_ref, turned_ref):
    turned_ref[...] = jnp.transpose(table_ref[...])
    table = jnp.concatenate([turned_ref[pl.ds(p, 8, stride=16), :] for p in range(16)], axis=1)
    high = table.astype(jnp.bfloat16).astype(jnp.float32)
    ones = jnp.ones((8, table.shape[1]), jnp.float32)
    for_high = jnp.concatenate([high, ones, table - high], axis=0).astype(jnp.bfloat16)
    for_low = jnp.concatenate([high, ones], axis=0).astype(jnp.bfloat16)
    sub = lax.broadcasted_iota(jnp.int32, (8, LANES), 0).astype(jnp.float32)

    def tile(row):
        lam = jnp.broadcast_to(lam_ref[pl.ds(row, 1), :], (8, LANES))
        curve = jnp.broadcast_to(curve_ref[pl.ds(row, 1), :], (8, LANES))
        mu = lam + curve
        ratio2 = jnp.exp(curve * (2.0 / (512.0 * 512.0)))
        columns = []
        for g in range(4):
            s = ((sub + 8.0 * g) * 16.0 + 0.5) * (1 / 512.0) - 0.5
            e = jnp.exp(mu * s + curve * (s * s))
            ratio = jnp.exp(mu * (1 / 512.0) + curve * ((2.0 * s + 1 / 512.0) * (1 / 512.0)))
            column = []
            for p in range(16):
                column.append(e)
                if p < 15:
                    e = e * ratio
                    ratio = ratio * ratio2
            columns.append(column)
        return jnp.concatenate([columns[g][p] for p in range(16) for g in range(4)], axis=0)

    def pair(row):
        e = jnp.concatenate([tile(row), tile(row + 1)], axis=1)
        e_high = e.astype(jnp.bfloat16)
        e_low = (e - e_high.astype(jnp.float32)).astype(jnp.bfloat16)
        sums = jnp.dot(for_high, e_high, preferred_element_type=jnp.float32)
        more = jnp.dot(for_low, e_low, preferred_element_type=jnp.float32)
        values = (sums[0:8] + sums[16:24] + more[0:8]) / (sums[8:16] + more[8:16])
        return [values[:, :LANES], values[:, LANES:]]

    def body(t, _):
        values = pair(4 * t) + pair(4 * t + 2)
        rows = pl.ds(pl.multiple_of(8 * t, 8), 8)
        for x in range(4):
            block = jnp.concatenate([v[2 * x : 2 * x + 2] for v in values], axis=0)
            for y in range(4):
                sent_ref[y, x, rows, :] = block
        return 0

    rows = lam_ref.shape[0]
    for x in range(4):
        for y in range(4):
            sent_ref[y, x, 2 * rows :, :] = lam_ref[...]
    lax.fori_loop(0, rows // 4, body, 0, unroll=16)


def species(lam, curve, table):
    rows = lam.shape[0]
    return pl.pallas_call(
        species_kernel,
        out_shape=jax.ShapeDtypeStruct((4, 4, 3 * rows, LANES), jnp.float32),
        in_specs=[pl.BlockSpec(memory_space=pltpu.VMEM)] * 3,
        out_specs=pl.BlockSpec(memory_space=pltpu.VMEM),
        scratch_shapes=[pltpu.VMEM((LANES, 32), jnp.float32)],
        cost_estimate=pl.CostEstimate(flops=6 * 10**9, bytes_accessed=1 << 19, transcendentals=0),
        compiler_params=pltpu.CompilerParams(vmem_limit_bytes=16 << 20),
        name="species",
    )(lam, curve, table)


def blocks_kernel(table_ref, out_ref, turned_ref):
    points = table_ref.shape[0]
    turned_ref[:, :points] = jnp.transpose(table_ref[...])
    block = [turned_ref[pl.ds(q, 8, stride=8), :points] for q in range(8)]
    block = jnp.concatenate(block, axis=1)
    out_ref[...] = jnp.broadcast_to(block[:, None, :], out_ref.shape)


def blocks(table):
    return pl.pallas_call(
        blocks_kernel,
        out_shape=jax.ShapeDtypeStruct((8, 4, LANES), jnp.float32),
        in_specs=[pl.BlockSpec(memory_space=pltpu.VMEM)],
        out_specs=pl.BlockSpec(memory_space=pltpu.VMEM),
        scratch_shapes=[pltpu.VMEM((64, LANES), jnp.float32)],
        compiler_params=pltpu.CompilerParams(vmem_limit_bytes=4 << 20),
        name="blocks",
    )(table)


def lay_kernel(flip, first, core_ref, blocks_ref, *refs):
    species_ref, lam_ref, sems = refs[-3:]
    rows = lam_ref.shape[3]
    core = core_ref[0] ^ flip
    here = pl.ds(first, blocks_ref.shape[0])
    copies = [
        (blocks_ref.at[:, :, pl.ds(0, 2 * rows), :], species_ref.at[here, core]),
        (blocks_ref.at[:, :, pl.ds(2 * rows, rows), :], lam_ref.at[here, core]),
    ]
    started = [pltpu.make_async_copy(a, b, sems.at[i]) for i, (a, b) in enumerate(copies)]
    for copy in started:
        copy.start()
    for copy in started:
        copy.wait()


def lay(core, blocks, flip, first=0, laid=()):
    anywhere = pl.BlockSpec(memory_space=pl.ANY)
    rows = blocks.shape[2] // 3
    return pl.pallas_call(
        functools.partial(lay_kernel, flip, first),
        out_shape=[
            jax.ShapeDtypeStruct((4, 2, 4, 2 * rows, LANES), jnp.float32),
            jax.ShapeDtypeStruct((4, 2, 4, rows, LANES), jnp.float32),
        ],
        in_specs=[pl.BlockSpec(memory_space=pltpu.SMEM), pl.BlockSpec(memory_space=pltpu.VMEM)]
        + [anywhere] * len(laid),
        out_specs=[anywhere] * 2,
        input_output_aliases={2: 0, 3: 1} if laid else {},
        scratch_shapes=[pltpu.SemaphoreType.DMA((2,))],
        cost_estimate=pl.CostEstimate(flops=2 * 10**9, bytes_accessed=3 << 20, transcendentals=0),
        compiler_params=pltpu.CompilerParams(vmem_limit_bytes=4 << 20),
        name="lay",
    )(core, blocks, *laid)


def exchange(array, axes):
    return lax.all_to_all(array, axes, split_axis=0, concat_axis=0, tiled=True)


def per_device(slope, curvature, target_mean, target_var, table):
    x = lax.axis_index("x")
    core = jnp.reshape(lax.axis_index("core"), (1,)).astype(jnp.int32)
    points = exchange(blocks(table.T).reshape(32, LANES), ("z", "x"))

    size = slope.shape[0] // 4
    mine = [
        lax.dynamic_slice_in_dim(a, x * size, size, 0).reshape(-1, LANES)
        for a in (slope, curvature, target_mean, target_var)
    ]
    lam = newton(*mine)
    sent = species(lam, mine[1], points)
    own = exchange(sent.reshape(16, *sent.shape[2:]), ("y", "x")).reshape(sent.shape)
    others = [lax.ppermute(own[y : y + 2], "core", [(0, 1), (1, 0)]) for y in (0, 2)]
    laid = lay(core, own, 0)
    laid = lay(core, others[0], 1, 0, laid)
    values, final_slope = lay(core, others[1], 1, 2, laid)
    values = jnp.transpose(values.reshape(-1, 2, LANES), (1, 0, 2)).reshape(2, -1)
    return values, final_slope.reshape(-1)


def solution(mesh):
    mesh = jax.sharding.Mesh(np.reshape(mesh.devices, (8, 4, 4, 2)), ("z", "x", "y", "core"))
    bins = P(("y", "core"))
    placed = (bins, bins, bins, bins, P(None, ("z", "x")))
    return jax.shard_map(
        per_device, mesh=mesh, in_specs=placed, out_specs=(P(("z", "x"), None), P()), check_vma=False
    )
```

```python
import functools

import jax
import jax.numpy as jnp
import numpy as np
from jax import lax
from jax.experimental import pallas as pl
from jax.experimental.pallas import tpu as pltpu
from jax.sharding import PartitionSpec as P

ITERS = 3
LANES = 128
EARLY = 6
COARSE = 8
FINE = 16


def weights(lam_ref, curve_ref, t):
    sub = lax.broadcasted_iota(jnp.int32, (8, LANES), 0).astype(jnp.float32)

    def tile(row):
        lam = jnp.broadcast_to(lam_ref[pl.ds(row, 1), :], (8, LANES))
        curve = jnp.broadcast_to(curve_ref[pl.ds(row, 1), :], (8, LANES))
        mu = lam + curve
        ratio2 = jnp.exp(curve * (2.0 / (512.0 * 512.0)))
        columns = []
        for g in range(4):
            s = ((sub + 8.0 * g) * 16.0 + 0.5) * (1 / 512.0) - 0.5
            e = jnp.exp(mu * s + curve * (s * s))
            ratio = jnp.exp(mu * (1 / 512.0) + curve * ((2.0 * s + 1 / 512.0) * (1 / 512.0)))
            column = []
            for p in range(16):
                column.append(e)
                if p < 15:
                    e = e * ratio
                    ratio = ratio * ratio2
            columns.append(column)
        return jnp.concatenate([columns[g][p] for p in range(16) for g in range(4)], axis=0)

    e = jnp.concatenate([tile(2 * t), tile(2 * t + 1)], axis=1)
    high = e.astype(jnp.bfloat16)
    return high, (e - high.astype(jnp.float32)).astype(jnp.bfloat16)


def newton_kernel(
    slope_ref, curve_ref, mean_ref, var_ref, lam_ref, high_ref, low_ref, ch_ref, sh_ref, g_ref
):
    def body(v, _):
        rows = pl.ds(pl.multiple_of(v * 8, 8), 8)
        curve = curve_ref[rows, :]
        mean = mean_ref[rows, :]
        inverse = 1.0 / var_ref[rows, :]
        for j in range(FINE):
            angle = curve * ((2 * j + 1) / 16384.0)
            up, down = jnp.exp(angle), jnp.exp(-angle)
            up2, down2 = up * up, down * down
            for i in range(COARSE):
                ch_ref[i * FINE + j] = 0.5 * (up + down)
                sh_ref[i * FINE + j] = 0.5 * (up - down)
                if i < COARSE - 1:
                    up, down = up * up2, down * down2
            g_ref[j] = jnp.exp(curve * (((2 * j + 1) / 1024.0) ** 2))
        for i in range(COARSE):
            g_ref[FINE + i] = jnp.exp(curve * (((2 * i + 1) / 32.0) ** 2))

        def newton(_, lam):
            mu = lam + curve
            up, down = jnp.exp(mu * (1 / 1024.0)), jnp.exp(mu * (-1 / 1024.0))
            up2, down2 = up * up, down * down
            sums = [[None] * 4 for _ in range(COARSE)]
            for j in range(FINE):
                g = g_ref[j]
                even, odd = g * (up + down), g * (up - down)
                d = (2 * j + 1) / 1024.0
                d_even, d_odd = even * d, odd * d
                for i in range(COARSE):
                    ch, sh = ch_ref[i * FINE + j], sh_ref[i * FINE + j]
                    terms = (ch * even, sh * odd, ch * d_odd, sh * d_even)
                    sums[i] = [t if s is None else s + t for s, t in zip(sums[i], terms)]
                if j < FINE - 1:
                    up, down = up * up2, down * down2
            up, down = jnp.exp(mu * (1 / 32.0)), jnp.exp(mu * (-1 / 32.0))
            up2, down2 = up * up, down * down
            partition, moment = 0.0, 0.0
            for i in range(COARSE):
                g = g_ref[FINE + i]
                even, odd = g * (up + down), g * (up - down)
                a = (2 * i + 1) / 32.0
                e0, o0, o1, e1 = sums[i]
                partition = partition + (even * e0 + odd * o0)
                moment = moment + (a * (odd * e0 + even * o0) + (even * o1 + odd * e1))
                if i < COARSE - 1:
                    up, down = up * up2, down * down2
            return lam + (mean - (0.5 + moment / partition)) * inverse

        lam_ref[rows, :] = lax.fori_loop(0, ITERS, newton, slope_ref[rows, :])
        return 0

    lax.fori_loop(0, lam_ref.shape[0] // 8, body, 0)

    def early(t, _):
        high_ref[t], low_ref[t] = weights(lam_ref, curve_ref, t)
        return 0

    lax.fori_loop(0, EARLY, early, 0, unroll=EARLY)


def newton(slope, curve, mean, var):
    part = jax.ShapeDtypeStruct((EARLY, 512, 2 * LANES), jnp.bfloat16)
    return pl.pallas_call(
        newton_kernel,
        out_shape=[jax.ShapeDtypeStruct(slope.shape, jnp.float32), part, part],
        in_specs=[pl.BlockSpec(memory_space=pltpu.VMEM)] * 4,
        out_specs=[pl.BlockSpec(memory_space=pltpu.VMEM)] * 3,
        scratch_shapes=[pltpu.VMEM((COARSE * FINE, 8, LANES), jnp.float32)] * 2
        + [pltpu.VMEM((COARSE + FINE, 8, LANES), jnp.float32)],
        cost_estimate=pl.CostEstimate(flops=12 * 10**9, bytes_accessed=1 << 18, transcendentals=0),
        compiler_params=pltpu.CompilerParams(vmem_limit_bytes=12 << 20),
        name="newton",
    )(slope, curve, mean, var)


def species_kernel(lam_ref, curve_ref, high_ref, low_ref, table_ref, sent_ref, turned_ref):
    turned_ref[...] = jnp.transpose(table_ref[...])
    table = jnp.concatenate([turned_ref[pl.ds(p, 8, stride=16), :] for p in range(16)], axis=1)
    high = table.astype(jnp.bfloat16).astype(jnp.float32)
    ones = jnp.ones((8, table.shape[1]), jnp.float32)
    for_high = jnp.concatenate([high, ones, table - high], axis=0).astype(jnp.bfloat16)
    for_low = jnp.concatenate([high, ones], axis=0).astype(jnp.bfloat16)
    def pair(high, low):
        sums = jnp.dot(for_high, high, preferred_element_type=jnp.float32)
        more = jnp.dot(for_low, low, preferred_element_type=jnp.float32)
        values = (sums[0:8] + sums[16:24] + more[0:8]) / (sums[8:16] + more[8:16])
        return [values[:, :LANES], values[:, LANES:]]

    def store(t, values):
        rows = pl.ds(pl.multiple_of(8 * t, 8), 8)
        for x in range(4):
            block = jnp.concatenate([v[2 * x : 2 * x + 2] for v in values], axis=0)
            for y in range(4):
                sent_ref[x, y, rows, :] = block

    def early(t, _):
        store(t, [v for n in (2 * t, 2 * t + 1) for v in pair(high_ref[n], low_ref[n])])
        return 0

    def late(t, _):
        pairs = (weights(lam_ref, curve_ref, 2 * t + n) for n in range(2))
        store(t, [v for p in pairs for v in pair(*p)])
        return 0

    rows = lam_ref.shape[0]
    for x in range(4):
        for y in range(4):
            sent_ref[x, y, 2 * rows :, :] = lam_ref[...]
    first = EARLY // 2
    lax.fori_loop(0, first, early, 0, unroll=first)
    lax.fori_loop(first, rows // 4, late, 0, unroll=13)


def species(lam, curve, early, table):
    rows = lam.shape[0]
    return pl.pallas_call(
        species_kernel,
        out_shape=jax.ShapeDtypeStruct((4, 4, 3 * rows, LANES), jnp.float32),
        in_specs=[pl.BlockSpec(memory_space=pltpu.VMEM)] * 5,
        out_specs=pl.BlockSpec(memory_space=pltpu.VMEM),
        scratch_shapes=[pltpu.VMEM((LANES, 32), jnp.float32)],
        cost_estimate=pl.CostEstimate(flops=6 * 10**9, bytes_accessed=1 << 19, transcendentals=0),
        compiler_params=pltpu.CompilerParams(vmem_limit_bytes=16 << 20),
        name="species",
    )(lam, curve, *early, table)


def blocks_kernel(table_ref, out_ref, turned_ref):
    points = table_ref.shape[0]
    turned_ref[:, :points] = jnp.transpose(table_ref[...])
    block = [turned_ref[pl.ds(q, 8, stride=8), :points] for q in range(8)]
    block = jnp.concatenate(block, axis=1)
    out_ref[...] = jnp.broadcast_to(block[:, None, :], out_ref.shape)


def blocks(table):
    return pl.pallas_call(
        blocks_kernel,
        out_shape=jax.ShapeDtypeStruct((8, 4, LANES), jnp.float32),
        in_specs=[pl.BlockSpec(memory_space=pltpu.VMEM)],
        out_specs=pl.BlockSpec(memory_space=pltpu.VMEM),
        scratch_shapes=[pltpu.VMEM((64, LANES), jnp.float32)],
        compiler_params=pltpu.CompilerParams(vmem_limit_bytes=4 << 20),
        name="blocks",
    )(table)


def lay_kernel(flip, core_ref, blocks_ref, *refs):
    species_ref, lam_ref, sems = refs[-3:]
    rows = lam_ref.shape[3]
    core = core_ref[0] ^ flip
    copies = []
    for y in range(4):
        copies.append((blocks_ref.at[:, y, pl.ds(0, 2 * rows), :], species_ref.at[y, core]))
        copies.append((blocks_ref.at[:, y, pl.ds(2 * rows, rows), :], lam_ref.at[y, core]))
    started = [pltpu.make_async_copy(a, b, sems.at[i]) for i, (a, b) in enumerate(copies)]
    for copy in started:
        copy.start()
    for copy in started:
        copy.wait()


def lay(core, blocks, flip, laid=()):
    anywhere = pl.BlockSpec(memory_space=pl.ANY)
    rows = blocks.shape[2] // 3
    return pl.pallas_call(
        functools.partial(lay_kernel, flip),
        out_shape=[
            jax.ShapeDtypeStruct((4, 2, 4, 2 * rows, LANES), jnp.float32),
            jax.ShapeDtypeStruct((4, 2, 4, rows, LANES), jnp.float32),
        ],
        in_specs=[pl.BlockSpec(memory_space=pltpu.SMEM), pl.BlockSpec(memory_space=pltpu.VMEM)]
        + [anywhere] * len(laid),
        out_specs=[anywhere] * 2,
        input_output_aliases={2: 0, 3: 1} if laid else {},
        scratch_shapes=[pltpu.SemaphoreType.DMA((8,))],
        cost_estimate=pl.CostEstimate(flops=2 * 10**9, bytes_accessed=3 << 20, transcendentals=0),
        compiler_params=pltpu.CompilerParams(vmem_limit_bytes=4 << 20),
        name="lay",
    )(core, blocks, *laid)


def exchange(array, axes):
    return lax.all_to_all(array, axes, split_axis=0, concat_axis=0, tiled=True)


def per_device(slope, curvature, target_mean, target_var, table):
    x = lax.axis_index("x")
    core = jnp.reshape(lax.axis_index("core"), (1,)).astype(jnp.int32)
    points = exchange(blocks(table.T).reshape(32, LANES), ("z", "x"))

    size = slope.shape[0] // 4
    mine = [
        lax.dynamic_slice_in_dim(a, x * size, size, 0).reshape(-1, LANES)
        for a in (slope, curvature, target_mean, target_var)
    ]
    lam, *early = newton(*mine)
    sent = species(lam, mine[1], early, points)
    own = exchange(sent.reshape(16, *sent.shape[2:]), ("x", "y")).reshape(sent.shape)
    other = lax.ppermute(own, "core", [(0, 1), (1, 0)])
    values, final_slope = lay(core, other, 1, lay(core, own, 0))
    values = jnp.transpose(values.reshape(-1, 2, LANES), (1, 0, 2)).reshape(2, -1)
    return values, final_slope.reshape(-1)


def solution(mesh):
    mesh = jax.sharding.Mesh(np.reshape(mesh.devices, (8, 4, 4, 2)), ("z", "x", "y", "core"))
    bins = P(("y", "core"))
    placed = (bins, bins, bins, bins, P(None, ("z", "x")))
    return jax.shard_map(
        per_device, mesh=mesh, in_specs=placed, out_specs=(P(("z", "x"), None), P()), check_vma=False
    )
```

```python
import functools

import jax
import jax.numpy as jnp
import numpy as np
from jax import lax
from jax.experimental import pallas as pl
from jax.experimental.pallas import tpu as pltpu
from jax.sharding import PartitionSpec as P

ITERS = 3
LANES = 128
COARSE = 8
FINE = 16


def newton_kernel(slope_ref, curve_ref, mean_ref, var_ref, lam_ref, ch_ref, sh_ref, g_ref):
    def body(v, _):
        rows = pl.ds(pl.multiple_of(v * 8, 8), 8)
        curve = curve_ref[rows, :]
        mean = mean_ref[rows, :]
        inverse = 1.0 / var_ref[rows, :]
        for j in range(FINE):
            angle = curve * ((2 * j + 1) / 16384.0)
            up, down = jnp.exp(angle), jnp.exp(-angle)
            up2, down2 = up * up, down * down
            for i in range(COARSE):
                ch_ref[i * FINE + j] = 0.5 * (up + down)
                sh_ref[i * FINE + j] = 0.5 * (up - down)
                if i < COARSE - 1:
                    up, down = up * up2, down * down2
            g_ref[j] = jnp.exp(curve * (((2 * j + 1) / 1024.0) ** 2))
        for i in range(COARSE):
            g_ref[FINE + i] = jnp.exp(curve * (((2 * i + 1) / 32.0) ** 2))

        def newton(_, lam):
            mu = lam + curve
            up, down = jnp.exp(mu * (1 / 1024.0)), jnp.exp(mu * (-1 / 1024.0))
            up2, down2 = up * up, down * down
            sums = [[None] * 4 for _ in range(COARSE)]
            for j in range(FINE):
                g = g_ref[j]
                even, odd = g * (up + down), g * (up - down)
                d = (2 * j + 1) / 1024.0
                d_even, d_odd = even * d, odd * d
                for i in range(COARSE):
                    ch, sh = ch_ref[i * FINE + j], sh_ref[i * FINE + j]
                    terms = (ch * even, sh * odd, ch * d_odd, sh * d_even)
                    sums[i] = [t if s is None else s + t for s, t in zip(sums[i], terms)]
                if j < FINE - 1:
                    up, down = up * up2, down * down2
            up, down = jnp.exp(mu * (1 / 32.0)), jnp.exp(mu * (-1 / 32.0))
            up2, down2 = up * up, down * down
            partition, moment = 0.0, 0.0
            for i in range(COARSE):
                g = g_ref[FINE + i]
                even, odd = g * (up + down), g * (up - down)
                a = (2 * i + 1) / 32.0
                e0, o0, o1, e1 = sums[i]
                partition = partition + (even * e0 + odd * o0)
                moment = moment + (a * (odd * e0 + even * o0) + (even * o1 + odd * e1))
                if i < COARSE - 1:
                    up, down = up * up2, down * down2
            return lam + (mean - (0.5 + moment / partition)) * inverse

        lam_ref[rows, :] = lax.fori_loop(0, ITERS, newton, slope_ref[rows, :], unroll=ITERS)
        return 0

    lax.fori_loop(0, lam_ref.shape[0] // 8, body, 0)


def newton(slope, curve, mean, var):
    return pl.pallas_call(
        newton_kernel,
        out_shape=jax.ShapeDtypeStruct(slope.shape, jnp.float32),
        in_specs=[pl.BlockSpec(memory_space=pltpu.VMEM)] * 4,
        out_specs=pl.BlockSpec(memory_space=pltpu.VMEM),
        scratch_shapes=[pltpu.VMEM((COARSE * FINE, 8, LANES), jnp.float32)] * 2
        + [pltpu.VMEM((COARSE + FINE, 8, LANES), jnp.float32)],
        cost_estimate=pl.CostEstimate(flops=12 * 10**9, bytes_accessed=1 << 18, transcendentals=0),
        compiler_params=pltpu.CompilerParams(vmem_limit_bytes=8 << 20),
        name="newton",
    )(slope, curve, mean, var)


def species_kernel(lam_ref, curve_ref, table_ref, sent_ref, turned_ref):
    turned_ref[...] = jnp.transpose(table_ref[...])
    table = jnp.concatenate([turned_ref[pl.ds(p, 8, stride=16), :] for p in range(16)], axis=1)
    high = table.astype(jnp.bfloat16).astype(jnp.float32)
    ones = jnp.ones((8, table.shape[1]), jnp.float32)
    for_high = jnp.concatenate([high, ones, table - high], axis=0).astype(jnp.bfloat16)
    for_low = jnp.concatenate([high, ones], axis=0).astype(jnp.bfloat16)
    sub = lax.broadcasted_iota(jnp.int32, (8, LANES), 0).astype(jnp.float32)

    def tile(row):
        lam = jnp.broadcast_to(lam_ref[pl.ds(row, 1), :], (8, LANES))
        curve = jnp.broadcast_to(curve_ref[pl.ds(row, 1), :], (8, LANES))
        mu = lam + curve
        ratio2 = jnp.exp(curve * (2.0 / (512.0 * 512.0)))
        columns = []
        for g in range(4):
            s = ((sub + 8.0 * g) * 16.0 + 0.5) * (1 / 512.0) - 0.5
            e = jnp.exp(mu * s + curve * (s * s))
            ratio = jnp.exp(mu * (1 / 512.0) + curve * ((2.0 * s + 1 / 512.0) * (1 / 512.0)))
            column = []
            for p in range(16):
                column.append(e)
                if p < 15:
                    e = e * ratio
                    ratio = ratio * ratio2
            columns.append(column)
        return jnp.concatenate([columns[g][p] for p in range(16) for g in range(4)], axis=0)

    def pair(row):
        e = jnp.concatenate([tile(row), tile(row + 1)], axis=1)
        e_high = e.astype(jnp.bfloat16)
        e_low = (e - e_high.astype(jnp.float32)).astype(jnp.bfloat16)
        sums = jnp.dot(for_high, e_high, preferred_element_type=jnp.float32)
        more = jnp.dot(for_low, e_low, preferred_element_type=jnp.float32)
        values = (sums[0:8] + sums[16:24] + more[0:8]) / (sums[8:16] + more[8:16])
        return [values[:, :LANES], values[:, LANES:]]

    def body(t, _):
        values = pair(4 * t) + pair(4 * t + 2)
        rows = pl.ds(pl.multiple_of(8 * t, 8), 8)
        for x in range(4):
            block = jnp.concatenate([v[2 * x : 2 * x + 2] for v in values], axis=0)
            for y in range(4):
                sent_ref[x, y, rows, :] = block
        return 0

    rows = lam_ref.shape[0]
    for x in range(4):
        for y in range(4):
            sent_ref[x, y, 2 * rows :, :] = lam_ref[...]
    lax.fori_loop(0, rows // 4, body, 0, unroll=16)


def species(lam, curve, table):
    rows = lam.shape[0]
    return pl.pallas_call(
        species_kernel,
        out_shape=jax.ShapeDtypeStruct((4, 4, 3 * rows, LANES), jnp.float32),
        in_specs=[pl.BlockSpec(memory_space=pltpu.VMEM)] * 3,
        out_specs=pl.BlockSpec(memory_space=pltpu.VMEM),
        scratch_shapes=[pltpu.VMEM((LANES, 32), jnp.float32)],
        cost_estimate=pl.CostEstimate(flops=6 * 10**9, bytes_accessed=1 << 19, transcendentals=0),
        compiler_params=pltpu.CompilerParams(vmem_limit_bytes=16 << 20),
        name="species",
    )(lam, curve, table)


def blocks_kernel(table_ref, out_ref, turned_ref):
    points = table_ref.shape[0]
    turned_ref[:, :points] = jnp.transpose(table_ref[...])
    block = [turned_ref[pl.ds(q, 8, stride=8), :points] for q in range(8)]
    block = jnp.concatenate(block, axis=1)
    out_ref[...] = jnp.broadcast_to(block[:, None, :], out_ref.shape)


def blocks(table):
    return pl.pallas_call(
        blocks_kernel,
        out_shape=jax.ShapeDtypeStruct((8, 4, LANES), jnp.float32),
        in_specs=[pl.BlockSpec(memory_space=pltpu.VMEM)],
        out_specs=pl.BlockSpec(memory_space=pltpu.VMEM),
        scratch_shapes=[pltpu.VMEM((64, LANES), jnp.float32)],
        compiler_params=pltpu.CompilerParams(vmem_limit_bytes=4 << 20),
        name="blocks",
    )(table)


def lay_kernel(flip, core_ref, blocks_ref, *refs):
    species_ref, lam_ref, sems = refs[-3:]
    rows = lam_ref.shape[3]
    core = core_ref[0] ^ flip
    copies = []
    for y in range(4):
        copies.append((blocks_ref.at[:, y, pl.ds(0, 2 * rows), :], species_ref.at[y, core]))
        copies.append((blocks_ref.at[:, y, pl.ds(2 * rows, rows), :], lam_ref.at[y, core]))
    started = [pltpu.make_async_copy(a, b, sems.at[i]) for i, (a, b) in enumerate(copies)]
    for copy in started:
        copy.start()
    for copy in started:
        copy.wait()


def lay(core, blocks, flip, laid=()):
    anywhere = pl.BlockSpec(memory_space=pl.ANY)
    rows = blocks.shape[2] // 3
    return pl.pallas_call(
        functools.partial(lay_kernel, flip),
        out_shape=[
            jax.ShapeDtypeStruct((4, 2, 4, 2 * rows, LANES), jnp.float32),
            jax.ShapeDtypeStruct((4, 2, 4, rows, LANES), jnp.float32),
        ],
        in_specs=[pl.BlockSpec(memory_space=pltpu.SMEM), pl.BlockSpec(memory_space=pltpu.VMEM)]
        + [anywhere] * len(laid),
        out_specs=[anywhere] * 2,
        input_output_aliases={2: 0, 3: 1} if laid else {},
        scratch_shapes=[pltpu.SemaphoreType.DMA((8,))],
        cost_estimate=pl.CostEstimate(flops=2 * 10**9, bytes_accessed=3 << 20, transcendentals=0),
        compiler_params=pltpu.CompilerParams(vmem_limit_bytes=4 << 20),
        name="lay",
    )(core, blocks, *laid)


def exchange(array, axes):
    return lax.all_to_all(array, axes, split_axis=0, concat_axis=0, tiled=True)


def per_device(slope, curvature, target_mean, target_var, table):
    x = lax.axis_index("x")
    core = jnp.reshape(lax.axis_index("core"), (1,)).astype(jnp.int32)
    points = exchange(blocks(table.T).reshape(32, LANES), ("z", "x"))

    size = slope.shape[0] // 4
    mine = [
        lax.dynamic_slice_in_dim(a, x * size, size, 0).reshape(-1, LANES)
        for a in (slope, curvature, target_mean, target_var)
    ]
    lam = newton(*mine)
    sent = species(lam, mine[1], points)
    own = exchange(sent.reshape(16, *sent.shape[2:]), ("x", "y")).reshape(sent.shape)
    other = lax.ppermute(own, "core", [(0, 1), (1, 0)])
    values, final_slope = lay(core, other, 1, lay(core, own, 0))
    values = jnp.transpose(values.reshape(-1, 2, LANES), (1, 0, 2)).reshape(2, -1)
    return values, final_slope.reshape(-1)


def solution(mesh):
    mesh = jax.sharding.Mesh(np.reshape(mesh.devices, (8, 4, 4, 2)), ("z", "x", "y", "core"))
    bins = P(("y", "core"))
    placed = (bins, bins, bins, bins, P(None, ("z", "x")))
    return jax.shard_map(
        per_device, mesh=mesh, in_specs=placed, out_specs=(P(("z", "x"), None), P()), check_vma=False
    )
```
